32 devices in a mesh: depth: 8 (over z, x), imgy: 2 (over y), imgx: 2 (over core).
Axes of the slice: x: 2, y: 2, z: 4, core: 2. Of those that a mesh axis runs over, the one named last changes fastest.
Arguments:
- volume: bfloat16 [128, 512, 1024], P('depth', 'imgy', 'imgx'), may hold values from -6 to 6
- tf_centers: float32 [4], replicated, may hold values from -2 to 2
- tf_widths: float32 [4], replicated, may hold values from 0.4 to 1.5
- tf_colors: float32 [3, 4], replicated, may hold values from 0.2 to 3
- tf_opacity: float32 [4], replicated, may hold values from 0.3 to 3
Outputs:
- frame: float32 [4, 2, 256, 1024], P(None, 'imgy', 'depth', 'imgx')
The draws below stay inside these ranges and needn't reach their ends.
All inputs are finite; a program needn't handle non-finite values.
Results may differ from the reference program's by a relative error of at most 0.0003.
Values may be sent and summed in bfloat16 or wider, within the bound.
A program may use at most 64 MiB of HBM per device.

```python
import math
import jax
import jax.numpy as jnp
from jax import lax

BY = 256
BUMPS = 4
Z = 128
Y = 512
X = 1024
TILES_Y = 2


def shard_levels(rng, dims, pieces, least, high):
    gain, own = 1.0, jax.random.fold_in(rng, 6)
    for position, parts in pieces:
        steps = jnp.exp(jax.random.uniform(jax.random.fold_in(own, position), (parts,), jnp.float32, least / len(pieces), high / len(pieces)))
        gain = gain * jnp.repeat(steps, dims[position] // parts).reshape([-1 if axis == position else 1 for axis in range(len(dims))])
    return gain


def gaussian(rng, extent, deviation, limit, shards=(), kind=jnp.bfloat16):
    result = jax.random.normal(rng, extent, jnp.float32) * deviation
    if len(shards) > 0:
        result = shard_levels(rng, extent, shards, -0.22, 0.18) * result
    return jnp.clip(result, min=-limit, max=limit).astype(kind)


def setup_inputs(seed: int = 0) -> dict:
    key_list = jax.random.split(jax.random.key(seed), 6)
    volume = gaussian(key_list[0], (Z, Y, X), 1.0, 6.0, ((0, 8), (1, 2), (2, 2)))
    tf_centers = jnp.clip(jax.random.uniform(key_list[1], (BUMPS,), jnp.float32, -2.0, 2.0), -2.0, 2.0)
    tf_widths = jnp.clip(jnp.exp(jax.random.uniform(key_list[2], (BUMPS,), jnp.float32, math.log(0.4), math.log(1.5))), 0.4, 1.5)
    tf_colors = jnp.clip(jax.random.uniform(key_list[3], (3, BUMPS), jnp.float32, 0.2, 3.0), 0.2, 3.0)
    tf_opacity = jnp.clip(jnp.exp(jax.random.uniform(key_list[4], (BUMPS,), jnp.float32, math.log(0.3), math.log(3.0))), 0.3, 3.0)
    return {"volume": volume, "tf_centers": tf_centers, "tf_widths": tf_widths, "tf_colors": tf_colors, "tf_opacity": tf_opacity}


def shading(middle, grad_depth, grad_rows, grad_cols, tf_centers, tf_widths, tf_colors, tf_opacity, ray_step):
    extinction = jnp.zeros_like(middle)
    emission = [jnp.zeros_like(middle), jnp.zeros_like(middle), jnp.zeros_like(middle)]
    for bump_index in range(tf_centers.shape[0]):
        offset = (middle - tf_centers[bump_index]) / tf_widths[bump_index]
        profile = jnp.exp(-offset * offset)
        extinction = extinction + tf_opacity[bump_index] * profile
        for channel in range(3):
            emission[channel] = emission[channel] + tf_colors[channel, bump_index] * profile
    gradient_norm = jnp.sqrt(grad_depth * grad_depth + grad_rows * grad_rows + grad_cols * grad_cols + 0.25)
    lighting = 0.3 + 0.7 * jnp.abs(grad_depth) / gradient_norm
    passing = jnp.exp(-ray_step * extinction)
    weight = (1.0 - passing) * lighting
    glowing = jnp.stack([emitted * weight for emitted in emission])
    return (glowing, passing)

def reference(volume, tf_centers, tf_widths, tf_colors, tf_opacity):
    depth_count = volume.shape[0]
    ray_step = 1.5 / depth_count
    rows_all = volume.shape[1]
    cols_all = volume.shape[2]

    def march_layer(carried, layer_index):
        color_sum, passed = carried
        middle = lax.dynamic_index_in_dim(volume, layer_index, 0, keepdims=False).astype(jnp.float32)
        before_index = jnp.maximum(layer_index - 1, 0).astype(jnp.int32)
        after_index = jnp.minimum(layer_index + 1, depth_count - 1).astype(jnp.int32)
        before = lax.dynamic_index_in_dim(volume, before_index, 0, keepdims=False).astype(jnp.float32)
        after = lax.dynamic_index_in_dim(volume, after_index, 0, keepdims=False).astype(jnp.float32)
        before = jnp.where(layer_index > 0, before, jnp.float32(0.0))
        after = jnp.where(layer_index < depth_count - 1, after, jnp.float32(0.0))
        grad_depth = 0.5 * (after - before)
        side = jnp.pad(middle, 1)
        grad_rows = 0.5 * (side[2:, 1:-1] - side[:-2, 1:-1])
        grad_cols = 0.5 * (side[1:-1, 2:] - side[1:-1, :-2])
        glowing, passing = shading(middle, grad_depth, grad_rows, grad_cols, tf_centers, tf_widths, tf_colors, tf_opacity, ray_step)
        return ((color_sum + passed[None] * glowing, passed * passing), None)
    start = (jnp.zeros((3, rows_all, cols_all), jnp.float32), jnp.ones((rows_all, cols_all), jnp.float32))
    final, unused = lax.scan(march_layer, start, jnp.arange(depth_count, dtype=jnp.int32))
    color_sum, passed = final
    frame = jnp.concatenate([color_sum, (1.0 - passed)[None]], axis=0)
    return frame.reshape(4, TILES_Y, BY, cols_all)
```

```python
import functools
import math

import jax
import jax.numpy as jnp
from jax import lax
from jax.experimental import pallas as pl
from jax.experimental.pallas import tpu as pltpu
from jax.sharding import PartitionSpec as P

LOG2E = math.log2(math.e)
RS = 16
CS = 128
CH = 32
AHEAD = 5
LAG = 3
SH = 128
MU = 4096.0
POWER = 240.0 / math.log2(1.0 + MU)
MESH = pl.DeviceIdType.MESH


def encode(v):
    return jnp.exp2(jnp.log2(1.0 + MU * v) * POWER - 120.0).astype(jnp.bfloat16)


def decode(y):
    return jnp.exp2((jnp.log2(y.astype(jnp.float32)) + 120.0) * (1.0 / POWER)) * (1.0 / MU) - (1.0 / MU)


def fill_bands(dcol, drow):
    k = lax.broadcasted_iota(jnp.int32, dcol.shape, 0)
    j = lax.broadcasted_iota(jnp.int32, dcol.shape, 1)
    dcol[...] = jnp.where(k == j + CS + 1, 1.0, jnp.where(k == j + CS - 1, -1.0, 0.0)).astype(dcol.dtype)
    i = lax.broadcasted_iota(jnp.int32, drow.shape, 0)
    k = lax.broadcasted_iota(jnp.int32, drow.shape, 1)
    drow[...] = jnp.where(k == i + RS + 1, 1.0, jnp.where(k == i + RS - 1, -1.0, 0.0)).astype(drow.dtype)


def total(colors, c):
    t = jnp.full((8, 128), colors[c, 0], jnp.float32)
    for k in range(1, 4):
        t = t + colors[c, k]
    return t


def fill_tables(tab, layers_all, centers, widths, colors, opacity):
    scale = 1.5 / layers_all * LOG2E
    for k in range(4):
        w = jnp.full((8, 128), widths[k], jnp.float32)
        o = jnp.full((8, 128), opacity[k], jnp.float32) * scale
        tab[k] = jnp.full((8, 128), centers[k], jnp.float32)
        tab[4 + k] = -LOG2E / (w * w)
        tab[8 + k] = jnp.log2(o)
        for c in range(3):
            tab[12 + 4 * c + k] = 0.7 * colors[c, k] / o / total(colors, c)


def slopes(r0, ext, flat, dcol, drow):
    layers, cols = ext.shape[0] - 2, ext.shape[2] - 2 * CS
    here = pl.ds(r0, SH)
    for z in range(layers):
        r = jnp.dot(
            drow[...], ext[1 + z, pl.ds(r0, SH + 2 * RS), CS : CS + cols], preferred_element_type=jnp.float32
        )
        flat[z, here, :] = r * r + 1.0
    for h in range(cols // 256):
        at = slice(h * 256, h * 256 + 256)
        left = ext[1 : layers + 1, pl.ds(r0 + RS, SH), h * 256 : h * 256 + 512].reshape(layers * SH, 512)
        c = jnp.dot(left, dcol[...], preferred_element_type=jnp.float32).reshape(layers, SH, 256)
        flat[:, here, at] = flat[:, here, at] + c * c


def table(tab, i):
    return jnp.concatenate([tab[i], tab[i]], axis=0)


def bumps_of(s, cen, quad, off):
    bump = []
    for k in range(4):
        u = s - cen[k]
        bump.append(jnp.exp2(u * u * quad[k] + off[k]))
    return bump, (bump[0] + bump[1]) + (bump[2] + bump[3])


def tinted(tab, ch, acc):
    m = [table(tab, 12 + 4 * ch + k) for k in range(4)]
    return (m[0] * acc[0] + m[1] * acc[1]) + (m[2] * acc[2] + m[3] * acc[3])


def march(r0, ext, flat, tab, part):
    layers, cols = ext.shape[0] - 2, ext.shape[2] - 2 * CS
    tiles = cols // 128

    def tile(t, _):
        q0 = pl.multiple_of(r0 + t // tiles * 16, 16)
        l0 = pl.multiple_of(t % tiles * 128, 128)
        rows, lanes = pl.ds(q0, 16), pl.ds(l0, 128)

        def plane(z):
            return ext[z, pl.ds(pl.multiple_of(q0 + RS, 16), 16), pl.ds(l0 + CS, 128)].astype(jnp.float32)

        cen, quad, off = [[table(tab, 4 * i + k) for k in range(4)] for i in range(3)]
        acc = [jnp.zeros((16, 128), jnp.float32) for _ in range(4)]
        expo = jnp.zeros((16, 128), jnp.float32)
        passed = jnp.ones((16, 128), jnp.float32)
        before, s = plane(0), plane(1)
        for z in range(layers):
            after = plane(z + 2)
            d = after - before
            light = jnp.abs(d) * lax.rsqrt(d * d + flat[z, rows, lanes]) + (0.3 / 0.7)
            bump, thick = bumps_of(s, cen, quad, off)
            expo = expo - thick
            later = jnp.exp2(expo)
            weight = (passed - later) * light
            for k in range(4):
                acc[k] = acc[k] + weight * bump[k]
            passed = later
            before, s = s, after
        for ch in range(3):
            part[ch, rows, lanes] = tinted(tab, ch, acc)
        part[3, rows, lanes] = passed
        return 0

    lax.fori_loop(0, CH // 16 * tiles, tile, 0, unroll=2)


def kernel(n, ny, nx, vol, cen_h, wid_h, col_h, opa_h, out, cen, wid, col, opa,
           ext, part, flat, dcol, drow, tab, rowbuf, rowgot, sendbuf, recvbuf,
           local_sem, fetch_sem, depth_send, depth_recv, side_send, side_recv, row_send, row_recv,
           swap_send, swap_recv):
    layers, rows, cols = vol.shape
    me, iy, ix = lax.axis_index("depth"), lax.axis_index("imgy"), lax.axis_index("imgx")
    piece = rows // n
    chunks = rows // CH
    rounds = n.bit_length() - 1
    early = piece == CH

    mid_z, mid_y, mid_x = pl.ds(1, layers), pl.ds(RS, rows), pl.ds(CS, cols)
    fetches = [pltpu.make_async_copy(a, b, fetch_sem.at[i]) for i, (a, b) in enumerate(
        ((cen_h, cen), (wid_h, wid), (col_h, col), (opa_h, opa)))]
    own = pltpu.make_async_copy(vol, ext.at[mid_z, mid_y, mid_x], local_sem)

    def bit(dev, k):
        return lax.rem(lax.div(dev, 2**k), 2)

    def partner(k):
        return me + (1 - 2 * bit(me, k)) * 2**k

    def order_of(dev):
        flips = [(1 - 2 * bit(dev, k)) * 2**k for k in range(rounds)]

        def order(j):
            if not early:
                return j
            p = dev
            for k in range(rounds):
                p = p + flips[k] * (1 - bit(j, k))
            return p

        return order

    order = order_of(me)
    order_there = [order_of(me + 1), order_of(me - 1)]

    barrier = pltpu.get_barrier_semaphore()

    def greet(dev):
        pl.semaphore_signal(barrier, inc=1, device_id=dev, device_id_type=MESH)

    for k in range(rounds):
        greet({"depth": partner(k)})
    peers = jnp.int32(rounds)
    other = me + 2 * bit(me, 0) - 1
    for name, at, there in (
        ("depth", other, jnp.logical_and(other >= 0, other < n)),
        ("imgy", iy - 1, iy > 0),
        ("imgy", iy + 1, iy < ny - 1),
        ("imgx", ix - 1, ix > 0),
        ("imgx", ix + 1, ix < nx - 1),
    ):
        pl.when(there)(lambda name=name, at=at: greet({name: at}))
        peers = peers + there.astype(jnp.int32)
    own.start()
    for copy in fetches:
        copy.start()

    def depth_copy(side, p, j):
        r0 = pl.multiple_of(p * CH, CH)
        return pltpu.make_async_remote_copy(
            src_ref=vol.at[pl.ds((layers - 1) * (1 - side), 1), pl.ds(r0, CH), :],
            dst_ref=ext.at[pl.ds((layers + 1) * side, 1), pl.ds(r0 + RS, CH), mid_x],
            send_sem=depth_send.at[side, j],
            recv_sem=depth_recv.at[side, j],
            device_id={"depth": me + 1 - 2 * side},
            device_id_type=MESH,
        )

    def side_copy(side):
        return pltpu.make_async_remote_copy(
            src_ref=vol.at[:, :, pl.ds((cols - CS) * (1 - side), CS)],
            dst_ref=ext.at[mid_z, mid_y, pl.ds((cols + CS) * side, CS)],
            send_sem=side_send.at[side],
            recv_sem=side_recv.at[side],
            device_id={"imgx": ix + 1 - 2 * side},
            device_id_type=MESH,
        )

    def row_copy(side):
        return pltpu.make_async_remote_copy(
            src_ref=rowbuf.at[side],
            dst_ref=rowgot.at[side],
            send_sem=row_send.at[side],
            recv_sem=row_recv.at[side],
            device_id={"imgy": iy + 1 - 2 * side},
            device_id_type=MESH,
        )

    def send_row(side):
        at, pick = (rows, RS - 1) if side == 0 else (RS, 0)
        edge = [ext[1 + z, at : at + RS, mid_x].astype(jnp.float32)[pick : pick + 1] for z in range(layers)]
        rowbuf[side] = jnp.concatenate(edge, axis=0).astype(jnp.bfloat16)
        row_copy(side).start()

    def place_row(side):
        row_copy(side).wait_recv()
        got = rowgot[side].astype(jnp.float32)
        at = (rows + RS) * side
        for z in range(layers):
            ext[1 + z, at : at + RS, mid_x] = jnp.broadcast_to(got[z : z + 1], (RS, cols)).astype(jnp.bfloat16)

    sends = (me < n - 1, me > 0)
    side_sends = (ix < nx - 1, ix > 0)
    row_sends = (iy < ny - 1, iy > 0)

    def start_halos(j):
        for s in range(2):
            pl.when(sends[s])(lambda s=s: depth_copy(s, order_there[s](j), j).start())

    def clear(region):
        region[...] = jnp.zeros(region.shape, region.dtype)

    for s in range(2):
        pl.when(jnp.logical_not(sends[1 - s]))(lambda s=s: clear(ext.at[pl.ds((layers + 1) * s, 1), mid_y, mid_x]))
        pl.when(jnp.logical_not(side_sends[1 - s]))(
            lambda s=s: clear(ext.at[mid_z, mid_y, pl.ds((cols + CS) * s, CS)]))
        pl.when(jnp.logical_not(row_sends[1 - s]))(
            lambda s=s: clear(ext.at[mid_z, pl.ds((rows + RS) * s, RS), mid_x]))
    fill_bands(dcol, drow)
    pl.semaphore_wait(barrier, peers)

    def first(j, _):
        start_halos(j)
        return 0

    for s in range(2):
        pl.when(side_sends[s])(lambda s=s: side_copy(s).start())
    lax.fori_loop(0, min(AHEAD, chunks), first, 0)
    own.wait()
    for s in range(2):
        pl.when(row_sends[s])(lambda s=s: send_row(s))
    for copy in fetches:
        copy.wait()
    fill_tables(tab, layers * n, cen, wid, col, opa)

    lanes = cols // 128

    def slot(p, k):
        return n - n // 2**k + p // 2 ** (k + 1)

    def swap_copy(p, k):
        at = slot(p, k)
        return pltpu.make_async_remote_copy(
            src_ref=sendbuf.at[at],
            dst_ref=recvbuf.at[at],
            send_sem=swap_send.at[at],
            recv_sem=swap_recv.at[at],
            device_id={"depth": partner(k)},
            device_id_type=MESH,
        )

    def each_tile(body):
        def tile(t, _):
            body(pl.ds(pl.multiple_of(t * 128, 128), 128))
            return 0

        lax.fori_loop(0, lanes, tile, 0)

    def rows_of(p):
        return pl.ds(pl.multiple_of(p * piece, piece), piece)

    def over(a, b):
        return [a[c] + a[3] * b[c] for c in range(3)] + [a[3] * b[3]]

    def merged(p, k, here):
        v = [part[ch, rows_of(p), here] for ch in range(4)]
        for done in range(k):
            got = [decode(recvbuf[slot(p, done), ch, :, here]) for ch in range(4)]
            got[3] = 1.0 - got[3]
            behind = bit(me, done) == 1
            a = [jnp.where(behind, g, m) for g, m in zip(got, v)]
            b = [jnp.where(behind, m, g) for g, m in zip(got, v)]
            v = over(a, b)
        return v

    def give_piece(p, k):
        for done in range(k):
            swap_copy(p, done).wait_recv()

        def body(here):
            v = merged(p, k, here)
            for ch in range(4):
                sendbuf[slot(p, k), ch, :, here] = encode(1.0 - v[3] if ch == 3 else v[ch])

        each_tile(body)
        swap_copy(p, k).start()

    def give(p):
        apart = me + p - 2 * sum(bit(me, k) * bit(p, k) * 2**k for k in range(rounds))
        for k in range(rounds):
            pl.when(jnp.logical_and(bit(apart, k) == 1, lax.rem(apart, 2**k) == 0))(lambda k=k: give_piece(p, k))

    def finish_own():
        for k in range(rounds):
            swap_copy(me, k).wait_recv()

        def body(here):
            v = merged(me, rounds, here)
            for ch in range(4):
                out[ch, 0, :, here] = 1.0 - v[3] if ch == 3 else v[ch] * total(col, ch)[:1]

        each_tile(body)

    for s in range(2):
        pl.when(side_sends[1 - s])(lambda s=s: side_copy(s).wait_recv())

    def slope(i, _):
        at = lax.rem(i + 1, rows // SH)
        for s in range(2):
            edge = at == (rows // SH - 1) * s
            pl.when(jnp.logical_and(row_sends[1 - s], edge))(lambda s=s: place_row(s))
        slopes(pl.multiple_of(at * SH, SH), ext, flat, dcol, drow)
        return 0

    lax.fori_loop(0, rows // SH, slope, 0)

    def chunk(j, _):
        p = order(j)
        pl.when(j + AHEAD < chunks)(lambda: start_halos(j + AHEAD))
        for s in range(2):
            pl.when(sends[1 - s])(lambda s=s: depth_copy(s, p, j).wait_recv())
        march(pl.multiple_of(p * CH, CH), ext, flat, tab, part)
        if early:
            pl.when(bit(j, 0) == 0)(lambda: give_piece(p, 0))
            pl.when(jnp.logical_and(j > LAG, lax.rem(j + LAG, 2) == 1))(lambda: give(order(j - LAG)))
        return 0

    lax.fori_loop(0, chunks, chunk, 0)

    if early:
        for j in range(n - LAG, n - 1):
            if j % 2 == 1:
                give(order(jnp.int32(j)))
    else:
        for k in range(rounds):

            def give_round(h, _, k=k):
                give_piece(me % 2**k + (1 - bit(me, k)) * 2**k + h * 2 ** (k + 1), k)
                return 0

            lax.fori_loop(0, n // 2 ** (k + 1), give_round, 0)
    finish_own()

    def finish(j, _):
        for s in range(2):
            pl.when(sends[s])(lambda s=s: depth_copy(s, j, j).wait_send())
        return 0

    lax.fori_loop(0, chunks, finish, 0)
    for s in range(2):
        pl.when(side_sends[s])(lambda s=s: side_copy(s).wait_send())
    for s in range(2):
        pl.when(row_sends[s])(lambda s=s: row_copy(s).wait_send())

    for k in range(rounds):

        def sent(h, _, k=k):
            swap_copy(h * 2 ** (k + 1), k).wait_send()
            return 0

        lax.fori_loop(0, n // 2 ** (k + 1), sent, 0)


def local(volume, cen, wid, col, opa):
    n, ny, nx = lax.axis_size("depth"), lax.axis_size("imgy"), lax.axis_size("imgx")
    layers, rows, cols = volume.shape
    piece = rows // n
    dma = pltpu.SemaphoreType.DMA
    return pl.pallas_call(
        functools.partial(kernel, n, ny, nx),
        out_shape=jax.ShapeDtypeStruct((4, 1, piece, cols), jnp.float32),
        in_specs=[pl.BlockSpec(memory_space=pltpu.HBM)] * 5,
        out_specs=pl.BlockSpec(memory_space=pltpu.VMEM),
        scratch_shapes=[
            *(pltpu.SMEM(a.shape, jnp.float32) for a in (cen, wid, col, opa)),
            pltpu.VMEM((layers + 2, rows + 2 * RS, cols + 2 * CS), jnp.bfloat16),
            pltpu.VMEM((4, rows, cols), jnp.float32),
            pltpu.VMEM((layers, rows, cols), jnp.float32),
            pltpu.VMEM((512, 256), jnp.bfloat16),
            pltpu.VMEM((SH, SH + 2 * RS), jnp.bfloat16),
            pltpu.VMEM((24, 8, 128), jnp.float32),
            pltpu.VMEM((2, layers, cols), jnp.bfloat16),
            pltpu.VMEM((2, layers, cols), jnp.bfloat16),
            pltpu.VMEM((n - 1, 4, piece, cols), jnp.bfloat16),
            pltpu.VMEM((n - 1, 4, piece, cols), jnp.bfloat16),
            dma,
            dma((4,)),
            dma((2, rows // CH)),
            dma((2, rows // CH)),
            dma((2,)),
            dma((2,)),
            dma((2,)),
            dma((2,)),
            dma((n - 1,)),
            dma((n - 1,)),
        ],
        compiler_params=pltpu.CompilerParams(
            vmem_limit_bytes=64 * 2**20, collective_id=0, has_side_effects=True
        ),
        name="march_swap",
    )(volume, cen, wid, col, opa)


def solution(mesh):
    return jax.shard_map(
        local,
        mesh=mesh,
        in_specs=(P("depth", "imgy", "imgx"), P(), P(), P(), P()),
        out_specs=P(None, "imgy", "depth", "imgx"),
        check_vma=False,
    )
```

```python
import functools
import math

import jax
import jax.numpy as jnp
from jax import lax
from jax.experimental import pallas as pl
from jax.experimental.pallas import tpu as pltpu
from jax.sharding import PartitionSpec as P

LOG2E = math.log2(math.e)
RS = 16
CS = 128
CH = 32
AHEAD = 8
TURN = (7, 5, 6, 4, 3, 1, 2, 0)
GIVE = 6
SH = 128
MU = 4096.0
POWER = 240.0 / math.log2(1.0 + MU)
MESH = pl.DeviceIdType.MESH


def encode(v):
    return jnp.exp2(jnp.log2(1.0 + MU * v) * POWER - 120.0).astype(jnp.bfloat16)


def decode(y):
    return jnp.exp2((jnp.log2(y.astype(jnp.float32)) + 120.0) * (1.0 / POWER)) * (1.0 / MU) - (1.0 / MU)


def fill_bands(dcol, drow):
    k = lax.broadcasted_iota(jnp.int32, dcol.shape, 0)
    j = lax.broadcasted_iota(jnp.int32, dcol.shape, 1)
    dcol[...] = jnp.where(k == j + CS + 1, 1.0, jnp.where(k == j + CS - 1, -1.0, 0.0)).astype(dcol.dtype)
    i = lax.broadcasted_iota(jnp.int32, drow.shape, 0)
    k = lax.broadcasted_iota(jnp.int32, drow.shape, 1)
    drow[...] = jnp.where(k == i + RS + 1, 1.0, jnp.where(k == i + RS - 1, -1.0, 0.0)).astype(drow.dtype)


def total(colors, c):
    t = jnp.full((8, 128), colors[c, 0], jnp.float32)
    for k in range(1, 4):
        t = t + colors[c, k]
    return t


def fill_tables(tab, layers_all, centers, widths, colors, opacity):
    scale = 1.5 / layers_all * LOG2E
    for k in range(4):
        w = jnp.full((8, 128), widths[k], jnp.float32)
        o = jnp.full((8, 128), opacity[k], jnp.float32) * scale
        tab[k] = jnp.full((8, 128), centers[k], jnp.float32)
        tab[4 + k] = -LOG2E / (w * w)
        tab[8 + k] = jnp.log2(o)
        for c in range(3):
            tab[12 + 4 * c + k] = 0.7 * colors[c, k] / o / total(colors, c)


def slopes(r0, ext, flat, dcol, drow):
    layers, cols = ext.shape[0] - 2, ext.shape[2] - 2 * CS
    here = pl.ds(r0, SH)
    for z in range(layers):
        r = jnp.dot(
            drow[...], ext[1 + z, pl.ds(r0, SH + 2 * RS), CS : CS + cols], preferred_element_type=jnp.float32
        )
        flat[z, here, :] = r * r + 1.0
    for h in range(cols // 256):
        at = slice(h * 256, h * 256 + 256)
        left = ext[1 : layers + 1, pl.ds(r0 + RS, SH), h * 256 : h * 256 + 512].reshape(layers * SH, 512)
        c = jnp.dot(left, dcol[...], preferred_element_type=jnp.float32).reshape(layers, SH, 256)
        flat[:, here, at] = flat[:, here, at] + c * c


def table(tab, i):
    return jnp.concatenate([tab[i], tab[i]], axis=0)


def bumps_of(s, cen, quad, off):
    bump = []
    for k in range(4):
        u = s - cen[k]
        bump.append(jnp.exp2(u * u * quad[k] + off[k]))
    return bump, (bump[0] + bump[1]) + (bump[2] + bump[3])


def tinted(tab, ch, acc):
    m = [table(tab, 12 + 4 * ch + k) for k in range(4)]
    return (m[0] * acc[0] + m[1] * acc[1]) + (m[2] * acc[2] + m[3] * acc[3])


def march(r0, ext, flat, tab, part):
    layers, cols = ext.shape[0] - 2, ext.shape[2] - 2 * CS
    tiles = cols // 128

    def tile(t, _):
        q0 = pl.multiple_of(r0 + t // tiles * 16, 16)
        l0 = pl.multiple_of(t % tiles * 128, 128)
        rows, lanes = pl.ds(q0, 16), pl.ds(l0, 128)

        def plane(z):
            return ext[z, pl.ds(pl.multiple_of(q0 + RS, 16), 16), pl.ds(l0 + CS, 128)].astype(jnp.float32)

        cen, quad, off = [[table(tab, 4 * i + k) for k in range(4)] for i in range(3)]
        acc = [jnp.zeros((16, 128), jnp.float32) for _ in range(4)]
        expo = jnp.zeros((16, 128), jnp.float32)
        passed = jnp.ones((16, 128), jnp.float32)
        before, s = plane(0), plane(1)
        for z in range(layers):
            after = plane(z + 2)
            d = after - before
            light = jnp.abs(d) * lax.rsqrt(d * d + flat[z, rows, lanes]) + (0.3 / 0.7)
            bump, thick = bumps_of(s, cen, quad, off)
            expo = expo - thick
            later = jnp.exp2(expo)
            weight = (passed - later) * light
            for k in range(4):
                acc[k] = acc[k] + weight * bump[k]
            passed = later
            before, s = s, after
        for ch in range(3):
            part[ch, rows, lanes] = tinted(tab, ch, acc)
        part[3, rows, lanes] = passed
        return 0

    lax.fori_loop(0, CH // 16 * tiles, tile, 0, unroll=2)


def kernel(n, ny, nx, vol, cen_h, wid_h, col_h, opa_h, out, cen, wid, col, opa,
           ext, part, flat, dcol, drow, tab, rowbuf, rowgot, nearbuf, neargot, farbuf, fargot,
           local_sem, fetch_sem, depth_send, depth_recv, side_send, side_recv, row_send, row_recv,
           near_send, near_recv, far_send, far_recv):
    layers, rows, cols = vol.shape
    me, iy, ix = lax.axis_index("depth"), lax.axis_index("imgy"), lax.axis_index("imgx")
    piece = rows // n
    chunks = rows // CH
    rounds = n.bit_length() - 1
    early = piece == CH and n == len(TURN)

    mid_z, mid_y, mid_x = pl.ds(1, layers), pl.ds(RS, rows), pl.ds(CS, cols)
    fetches = [pltpu.make_async_copy(a, b, fetch_sem.at[i]) for i, (a, b) in enumerate(
        ((cen_h, cen), (wid_h, wid), (col_h, col), (opa_h, opa)))]
    own = pltpu.make_async_copy(vol, ext.at[mid_z, mid_y, mid_x], local_sem)

    def bit(dev, k):
        return lax.rem(lax.div(dev, 2**k), 2)

    def partner(k):
        return me + (1 - 2 * bit(me, k)) * 2**k

    def member(g):
        return me + sum((1 - 2 * bit(me, k)) * 2**k for k in range(2) if g >> k & 1)

    def away(dev, flips, mask):
        return dev + sum(flips[k] * bit(mask, k) for k in range(rounds))

    def order_of(dev):
        flips = [(1 - 2 * bit(dev, k)) * 2**k for k in range(rounds)]

        def order(j):
            if not early:
                return j
            mask = sum((j == i).astype(jnp.int32) * turn for i, turn in enumerate(TURN))
            return away(dev, flips, mask)

        return order

    order = order_of(me)
    order_there = [order_of(me + 1), order_of(me - 1)]

    barrier = pltpu.get_barrier_semaphore()

    def greet(dev):
        pl.semaphore_signal(barrier, inc=1, device_id=dev, device_id_type=MESH)

    for g in range(1, 4):
        greet({"depth": member(g)})
    for k in range(2, rounds):
        greet({"depth": partner(k)})
    peers = jnp.int32(rounds + 1)
    other = me + 2 * bit(me, 0) - 1
    for name, at, there in (
        ("depth", other, jnp.logical_and(other >= 0, other < n)),
        ("imgy", iy - 1, iy > 0),
        ("imgy", iy + 1, iy < ny - 1),
        ("imgx", ix - 1, ix > 0),
        ("imgx", ix + 1, ix < nx - 1),
    ):
        pl.when(there)(lambda name=name, at=at: greet({name: at}))
        peers = peers + there.astype(jnp.int32)
    own.start()
    for copy in fetches:
        copy.start()

    def depth_copy(side, p, j):
        r0 = pl.multiple_of(p * CH, CH)
        return pltpu.make_async_remote_copy(
            src_ref=vol.at[pl.ds((layers - 1) * (1 - side), 1), pl.ds(r0, CH), :],
            dst_ref=ext.at[pl.ds((layers + 1) * side, 1), pl.ds(r0 + RS, CH), mid_x],
            send_sem=depth_send.at[side, j],
            recv_sem=depth_recv.at[side, j],
            device_id={"depth": me + 1 - 2 * side},
            device_id_type=MESH,
        )

    def side_copy(side):
        return pltpu.make_async_remote_copy(
            src_ref=vol.at[:, :, pl.ds((cols - CS) * (1 - side), CS)],
            dst_ref=ext.at[mid_z, mid_y, pl.ds((cols + CS) * side, CS)],
            send_sem=side_send.at[side],
            recv_sem=side_recv.at[side],
            device_id={"imgx": ix + 1 - 2 * side},
            device_id_type=MESH,
        )

    def row_copy(side):
        return pltpu.make_async_remote_copy(
            src_ref=rowbuf.at[side],
            dst_ref=rowgot.at[side],
            send_sem=row_send.at[side],
            recv_sem=row_recv.at[side],
            device_id={"imgy": iy + 1 - 2 * side},
            device_id_type=MESH,
        )

    def send_row(side):
        at, pick = (rows, RS - 1) if side == 0 else (RS, 0)
        edge = [ext[1 + z, at : at + RS, mid_x].astype(jnp.float32)[pick : pick + 1] for z in range(layers)]
        rowbuf[side] = jnp.concatenate(edge, axis=0).astype(jnp.bfloat16)
        row_copy(side).start()

    def place_row(side):
        row_copy(side).wait_recv()
        got = rowgot[side].astype(jnp.float32)
        at = (rows + RS) * side
        for z in range(layers):
            ext[1 + z, at : at + RS, mid_x] = jnp.broadcast_to(got[z : z + 1], (RS, cols)).astype(jnp.bfloat16)

    sends = (me < n - 1, me > 0)
    side_sends = (ix < nx - 1, ix > 0)
    row_sends = (iy < ny - 1, iy > 0)

    def start_halos(j):
        for s in range(2):
            pl.when(sends[s])(lambda s=s: depth_copy(s, order_there[s](j), j).start())

    def clear(region):
        region[...] = jnp.zeros(region.shape, region.dtype)

    for s in range(2):
        pl.when(jnp.logical_not(sends[1 - s]))(lambda s=s: clear(ext.at[pl.ds((layers + 1) * s, 1), mid_y, mid_x]))
        pl.when(jnp.logical_not(side_sends[1 - s]))(
            lambda s=s: clear(ext.at[mid_z, mid_y, pl.ds((cols + CS) * s, CS)]))
        pl.when(jnp.logical_not(row_sends[1 - s]))(
            lambda s=s: clear(ext.at[mid_z, pl.ds((rows + RS) * s, RS), mid_x]))
    fill_bands(dcol, drow)
    pl.semaphore_wait(barrier, peers)

    def first(j, _):
        start_halos(j)
        return 0

    for s in range(2):
        pl.when(side_sends[s])(lambda s=s: side_copy(s).start())
    lax.fori_loop(0, min(AHEAD, chunks), first, 0)
    own.wait()
    for s in range(2):
        pl.when(row_sends[s])(lambda s=s: send_row(s))
    for copy in fetches:
        copy.wait()
    fill_tables(tab, layers * n, cen, wid, col, opa)

    lanes = cols // 128

    def near_copy(p, g):
        at = lax.div(p, 4)
        return pltpu.make_async_remote_copy(
            src_ref=nearbuf.at[g - 1, at],
            dst_ref=neargot.at[g - 1, at],
            send_sem=near_send.at[g - 1, at],
            recv_sem=near_recv.at[g - 1, at],
            device_id={"depth": member(g)},
            device_id_type=MESH,
        )

    def slot(p, k):
        return n // 4 - n // 2**k + lax.div(p, 2 ** (k + 1))

    def far_copy(p, k):
        at = slot(p, k)
        return pltpu.make_async_remote_copy(
            src_ref=farbuf.at[at],
            dst_ref=fargot.at[at],
            send_sem=far_send.at[at],
            recv_sem=far_recv.at[at],
            device_id={"depth": partner(k)},
            device_id_type=MESH,
        )

    def each_tile(body):
        def tile(t, _):
            body(pl.ds(pl.multiple_of(t * 128, 128), 128))
            return 0

        lax.fori_loop(0, lanes, tile, 0)

    def rows_of(p):
        return pl.ds(pl.multiple_of(p * piece, piece), piece)

    def over(a, b):
        return [a[c] + a[3] * b[c] for c in range(3)] + [a[3] * b[3]]

    def coded(ref, here, v):
        for ch in range(4):
            ref[ch, :, here] = encode(1.0 - v[3] if ch == 3 else v[ch])

    def decoded(ref, here):
        v = [decode(ref[ch, :, here]) for ch in range(4)]
        return v[:3] + [1.0 - v[3]]

    def join(k, held, got):
        behind = bit(me, k) == 1
        a = [jnp.where(behind, g, m) for g, m in zip(got, held)]
        b = [jnp.where(behind, m, g) for g, m in zip(got, held)]
        return over(a, b)

    def own_part(p, here):
        return [part[ch, rows_of(p), here] for ch in range(4)]

    def merged(p, k, here):
        near = [decoded(neargot.at[g, lax.div(p, 4)], here) for g in range(3)]
        v = join(1, join(0, own_part(p, here), near[0]), join(0, near[1], near[2]))
        for done in range(2, k):
            v = join(done, v, decoded(fargot.at[slot(p, done)], here))
        return v

    def gathered(p, k):
        for g in range(1, 4):
            near_copy(p, g).wait_recv()
        for done in range(2, k):
            far_copy(p, done).wait_recv()

    def near_send_piece(p, g):
        each_tile(lambda here: coded(nearbuf.at[g - 1, lax.div(p, 4)], here, own_part(p, here)))
        near_copy(p, g).start()

    def far_send_piece(p, k):
        gathered(p, k)
        each_tile(lambda here: coded(farbuf.at[slot(p, k)], here, merged(p, k, here)))
        far_copy(p, k).start()

    def finish_own():
        gathered(me, rounds)

        def body(here):
            v = merged(me, rounds, here)
            for ch in range(4):
                out[ch, 0, :, here] = 1.0 - v[3] if ch == 3 else v[ch] * total(col, ch)[:1]

        each_tile(body)

    for s in range(2):
        pl.when(side_sends[1 - s])(lambda s=s: side_copy(s).wait_recv())

    def slope(i, _):
        at = lax.rem(i + 1, rows // SH)
        for s in range(2):
            edge = at == (rows // SH - 1) * s
            pl.when(jnp.logical_and(row_sends[1 - s], edge))(lambda s=s: place_row(s))
        slopes(pl.multiple_of(at * SH, SH), ext, flat, dcol, drow)
        return 0

    lax.fori_loop(0, rows // SH, slope, 0)

    def chunk(j, _):
        p = order(j)
        pl.when(j + AHEAD < chunks)(lambda: start_halos(j + AHEAD))
        for s in range(2):
            pl.when(sends[1 - s])(lambda s=s: depth_copy(s, p, j).wait_recv())
        march(pl.multiple_of(p * CH, CH), ext, flat, tab, part)
        if early:
            for g in range(1, 4):
                turns = [i for i, turn in enumerate(TURN) if turn % 4 == g]
                pl.when(functools.reduce(jnp.logical_or, [j == i for i in turns]))(lambda g=g: near_send_piece(p, g))
            pl.when(j == GIVE)(lambda: far_send_piece(me + 4 - 8 * bit(me, 2), 2))
        return 0

    lax.fori_loop(0, chunks, chunk, 0)

    if not early:
        for g in range(1, 4):

            def near(h, _, g=g):
                near_send_piece(lax.rem(member(g), 4) + h * 4, g)
                return 0

            lax.fori_loop(0, n // 4, near, 0)
        for k in range(2, rounds):

            def far(h, _, k=k):
                far_send_piece(lax.rem(me, 2**k) + (1 - bit(me, k)) * 2**k + h * 2 ** (k + 1), k)
                return 0

            lax.fori_loop(0, n // 2 ** (k + 1), far, 0)
    finish_own()

    def finish(j, _):
        for s in range(2):
            pl.when(sends[s])(lambda s=s: depth_copy(s, j, j).wait_send())
        return 0

    lax.fori_loop(0, chunks, finish, 0)
    for s in range(2):
        pl.when(side_sends[s])(lambda s=s: side_copy(s).wait_send())
    for s in range(2):
        pl.when(row_sends[s])(lambda s=s: row_copy(s).wait_send())

    def near_sent(h, _):
        for g in range(1, 4):
            near_copy(h * 4, g).wait_send()
        return 0

    lax.fori_loop(0, n // 4, near_sent, 0)
    for k in range(2, rounds):

        def far_sent(h, _, k=k):
            far_copy(h * 2 ** (k + 1), k).wait_send()
            return 0

        lax.fori_loop(0, n // 2 ** (k + 1), far_sent, 0)


def local(volume, cen, wid, col, opa):
    n, ny, nx = lax.axis_size("depth"), lax.axis_size("imgy"), lax.axis_size("imgx")
    layers, rows, cols = volume.shape
    piece = rows // n
    dma = pltpu.SemaphoreType.DMA
    return pl.pallas_call(
        functools.partial(kernel, n, ny, nx),
        out_shape=pltpu.VMEM((4, 1, piece, cols), jnp.float32),
        in_specs=[pl.BlockSpec(memory_space=pltpu.HBM)] * 5,
        out_specs=pl.BlockSpec(memory_space=pltpu.VMEM),
        scratch_shapes=[
            *(pltpu.SMEM(a.shape, jnp.float32) for a in (cen, wid, col, opa)),
            pltpu.VMEM((layers + 2, rows + 2 * RS, cols + 2 * CS), jnp.bfloat16),
            pltpu.VMEM((4, rows, cols), jnp.float32),
            pltpu.VMEM((layers, rows, cols), jnp.float32),
            pltpu.VMEM((512, 256), jnp.bfloat16),
            pltpu.VMEM((SH, SH + 2 * RS), jnp.bfloat16),
            pltpu.VMEM((24, 8, 128), jnp.float32),
            pltpu.VMEM((2, layers, cols), jnp.bfloat16),
            pltpu.VMEM((2, layers, cols), jnp.bfloat16),
            pltpu.VMEM((3, n // 4, 4, piece, cols), jnp.bfloat16),
            pltpu.VMEM((3, n // 4, 4, piece, cols), jnp.bfloat16),
            pltpu.VMEM((n // 4 - 1, 4, piece, cols), jnp.bfloat16),
            pltpu.VMEM((n // 4 - 1, 4, piece, cols), jnp.bfloat16),
            dma,
            dma((4,)),
            dma((2, rows // CH)),
            dma((2, rows // CH)),
            dma((2,)),
            dma((2,)),
            dma((2,)),
            dma((2,)),
            dma((3, n // 4)),
            dma((3, n // 4)),
            dma((n // 4 - 1,)),
            dma((n // 4 - 1,)),
        ],
        compiler_params=pltpu.CompilerParams(
            vmem_limit_bytes=63 * 2**20, collective_id=0, has_side_effects=True
        ),
        name="march_swap",
    )(volume, cen, wid, col, opa)


def solution(mesh):
    return jax.shard_map(
        local,
        mesh=mesh,
        in_specs=(P("depth", "imgy", "imgx"), P(), P(), P(), P()),
        out_specs=P(None, "imgy", "depth", "imgx"),
        check_vma=False,
    )
```

```python
import functools
import math

import jax
import jax.numpy as jnp
from jax import lax
from jax.experimental import pallas as pl
from jax.experimental.pallas import tpu as pltpu
from jax.sharding import PartitionSpec as P

LOG2E = math.log2(math.e)
RS = 16
CS = 128
CH = 32
AHEAD = 8
TURN = (7, 5, 6, 4, 2, 3, 1, 0)
GIVE = 5
SH = 128
MU = 4096.0
POWER = 240.0 / math.log2(1.0 + MU)
MESH = pl.DeviceIdType.MESH


def encode(v):
    return jnp.exp2(jnp.log2(1.0 + MU * v) * POWER - 120.0).astype(jnp.bfloat16)


def decode(y):
    return jnp.exp2((jnp.log2(y.astype(jnp.float32)) + 120.0) * (1.0 / POWER)) * (1.0 / MU) - (1.0 / MU)


def fill_bands(dcol, drow):
    k = lax.broadcasted_iota(jnp.int32, dcol.shape, 0)
    j = lax.broadcasted_iota(jnp.int32, dcol.shape, 1)
    dcol[...] = jnp.where(k == j + CS + 1, 1.0, jnp.where(k == j + CS - 1, -1.0, 0.0)).astype(dcol.dtype)
    i = lax.broadcasted_iota(jnp.int32, drow.shape, 0)
    k = lax.broadcasted_iota(jnp.int32, drow.shape, 1)
    drow[...] = jnp.where(k == i + RS + 1, 1.0, jnp.where(k == i + RS - 1, -1.0, 0.0)).astype(drow.dtype)


def total(colors, c):
    t = jnp.full((8, 128), colors[c, 0], jnp.float32)
    for k in range(1, 4):
        t = t + colors[c, k]
    return t


def fill_tables(tab, layers_all, centers, widths, colors, opacity):
    scale = 1.5 / layers_all * LOG2E
    for k in range(4):
        w = jnp.full((8, 128), widths[k], jnp.float32)
        o = jnp.full((8, 128), opacity[k], jnp.float32) * scale
        tab[k] = jnp.full((8, 128), centers[k], jnp.float32)
        tab[4 + k] = -LOG2E / (w * w)
        tab[8 + k] = jnp.log2(o)
        for c in range(3):
            tab[12 + 4 * c + k] = 0.7 * colors[c, k] / o / total(colors, c)


def slopes(r0, ext, flat, dcol, drow):
    layers, cols = ext.shape[0] - 2, ext.shape[2] - 2 * CS
    here = pl.ds(r0, SH)
    for z in range(layers):
        r = jnp.dot(
            drow[...], ext[1 + z, pl.ds(r0, SH + 2 * RS), CS : CS + cols], preferred_element_type=jnp.float32
        )
        flat[z, here, :] = r * r + 1.0
    for h in range(cols // 256):
        at = slice(h * 256, h * 256 + 256)
        left = ext[1 : layers + 1, pl.ds(r0 + RS, SH), h * 256 : h * 256 + 512].reshape(layers * SH, 512)
        c = jnp.dot(left, dcol[...], preferred_element_type=jnp.float32).reshape(layers, SH, 256)
        flat[:, here, at] = flat[:, here, at] + c * c


def table(tab, i):
    return jnp.concatenate([tab[i], tab[i]], axis=0)


def bumps_of(s, cen, quad, off):
    bump = []
    for k in range(4):
        u = s - cen[k]
        bump.append(jnp.exp2(u * u * quad[k] + off[k]))
    return bump, (bump[0] + bump[1]) + (bump[2] + bump[3])


def tinted(tab, ch, acc):
    m = [table(tab, 12 + 4 * ch + k) for k in range(4)]
    return (m[0] * acc[0] + m[1] * acc[1]) + (m[2] * acc[2] + m[3] * acc[3])


def march(r0, ext, flat, tab, part):
    layers, cols = ext.shape[0] - 2, ext.shape[2] - 2 * CS
    tiles = cols // 128

    def tile(t, _):
        q0 = pl.multiple_of(r0 + t // tiles * 16, 16)
        l0 = pl.multiple_of(t % tiles * 128, 128)
        rows, lanes = pl.ds(q0, 16), pl.ds(l0, 128)

        def plane(z):
            return ext[z, pl.ds(pl.multiple_of(q0 + RS, 16), 16), pl.ds(l0 + CS, 128)].astype(jnp.float32)

        cen, quad, off = [[table(tab, 4 * i + k) for k in range(4)] for i in range(3)]
        acc = [jnp.zeros((16, 128), jnp.float32) for _ in range(4)]
        expo = jnp.zeros((16, 128), jnp.float32)
        passed = jnp.ones((16, 128), jnp.float32)
        before, s = plane(0), plane(1)
        for z in range(layers):
            after = plane(z + 2)
            d = after - before
            light = jnp.abs(d) * lax.rsqrt(d * d + flat[z, rows, lanes]) + (0.3 / 0.7)
            bump, thick = bumps_of(s, cen, quad, off)
            expo = expo - thick
            later = jnp.exp2(expo)
            weight = (passed - later) * light
            for k in range(4):
                acc[k] = acc[k] + weight * bump[k]
            passed = later
            before, s = s, after
        for ch in range(3):
            part[ch, rows, lanes] = tinted(tab, ch, acc)
        part[3, rows, lanes] = passed
        return 0

    lax.fori_loop(0, CH // 16 * tiles, tile, 0, unroll=2)


def kernel(n, ny, nx, vol, cen_h, wid_h, col_h, opa_h, out, cen, wid, col, opa,
           ext, part, flat, dcol, drow, tab, rowbuf, rowgot, nearbuf, neargot, farbuf, fargot,
           local_sem, fetch_sem, depth_send, depth_recv, side_send, side_recv, row_send, row_recv,
           near_send, near_recv, far_send, far_recv):
    layers, rows, cols = vol.shape
    me, iy, ix = lax.axis_index("depth"), lax.axis_index("imgy"), lax.axis_index("imgx")
    piece = rows // n
    chunks = rows // CH
    rounds = n.bit_length() - 1
    early = piece == CH and n == len(TURN)

    mid_z, mid_y, mid_x = pl.ds(1, layers), pl.ds(RS, rows), pl.ds(CS, cols)
    fetches = [pltpu.make_async_copy(a, b, fetch_sem.at[i]) for i, (a, b) in enumerate(
        ((cen_h, cen), (wid_h, wid), (col_h, col), (opa_h, opa)))]
    own = pltpu.make_async_copy(vol, ext.at[mid_z, mid_y, mid_x], local_sem)

    def bit(dev, k):
        return lax.rem(lax.div(dev, 2**k), 2)

    def partner(k):
        return me + (1 - 2 * bit(me, k)) * 2**k

    def member(g):
        return me + sum((1 - 2 * bit(me, k)) * 2**k for k in range(2) if g >> k & 1)

    def away(dev, flips, mask):
        return dev + sum(flips[k] * bit(mask, k) for k in range(rounds))

    def order_of(dev):
        flips = [(1 - 2 * bit(dev, k)) * 2**k for k in range(rounds)]

        def order(j):
            if not early:
                return j
            mask = sum((j == i).astype(jnp.int32) * turn for i, turn in enumerate(TURN))
            return away(dev, flips, mask)

        return order

    order = order_of(me)
    order_there = [order_of(me + 1), order_of(me - 1)]

    barrier = pltpu.get_barrier_semaphore()

    def greet(dev):
        pl.semaphore_signal(barrier, inc=1, device_id=dev, device_id_type=MESH)

    for g in range(1, 4):
        greet({"depth": member(g)})
    for k in range(2, rounds):
        greet({"depth": partner(k)})
    peers = jnp.int32(rounds + 1)
    other = me + 2 * bit(me, 0) - 1
    for name, at, there in (
        ("depth", other, jnp.logical_and(other >= 0, other < n)),
        ("imgy", iy - 1, iy > 0),
        ("imgy", iy + 1, iy < ny - 1),
        ("imgx", ix - 1, ix > 0),
        ("imgx", ix + 1, ix < nx - 1),
    ):
        pl.when(there)(lambda name=name, at=at: greet({name: at}))
        peers = peers + there.astype(jnp.int32)
    own.start()
    for copy in fetches:
        copy.start()

    def depth_copy(side, p, j):
        r0 = pl.multiple_of(p * CH, CH)
        return pltpu.make_async_remote_copy(
            src_ref=vol.at[pl.ds((layers - 1) * (1 - side), 1), pl.ds(r0, CH), :],
            dst_ref=ext.at[pl.ds((layers + 1) * side, 1), pl.ds(r0 + RS, CH), mid_x],
            send_sem=depth_send.at[side, j],
            recv_sem=depth_recv.at[side, j],
            device_id={"depth": me + 1 - 2 * side},
            device_id_type=MESH,
        )

    def side_copy(side):
        return pltpu.make_async_remote_copy(
            src_ref=vol.at[:, :, pl.ds((cols - CS) * (1 - side), CS)],
            dst_ref=ext.at[mid_z, mid_y, pl.ds((cols + CS) * side, CS)],
            send_sem=side_send.at[side],
            recv_sem=side_recv.at[side],
            device_id={"imgx": ix + 1 - 2 * side},
            device_id_type=MESH,
        )

    def row_copy(side):
        return pltpu.make_async_remote_copy(
            src_ref=rowbuf.at[side],
            dst_ref=rowgot.at[side],
            send_sem=row_send.at[side],
            recv_sem=row_recv.at[side],
            device_id={"imgy": iy + 1 - 2 * side},
            device_id_type=MESH,
        )

    def send_row(side):
        at, pick = (rows, RS - 1) if side == 0 else (RS, 0)
        edge = [ext[1 + z, at : at + RS, mid_x].astype(jnp.float32)[pick : pick + 1] for z in range(layers)]
        rowbuf[side] = jnp.concatenate(edge, axis=0).astype(jnp.bfloat16)
        row_copy(side).start()

    def place_row(side):
        row_copy(side).wait_recv()
        got = rowgot[side].astype(jnp.float32)
        at = (rows + RS) * side
        for z in range(layers):
            ext[1 + z, at : at + RS, mid_x] = jnp.broadcast_to(got[z : z + 1], (RS, cols)).astype(jnp.bfloat16)

    sends = (me < n - 1, me > 0)
    side_sends = (ix < nx - 1, ix > 0)
    row_sends = (iy < ny - 1, iy > 0)

    def start_halos(j):
        for s in range(2):
            pl.when(sends[s])(lambda s=s: depth_copy(s, order_there[s](j), j).start())

    def clear(region):
        region[...] = jnp.zeros(region.shape, region.dtype)

    for s in range(2):
        pl.when(jnp.logical_not(sends[1 - s]))(lambda s=s: clear(ext.at[pl.ds((layers + 1) * s, 1), mid_y, mid_x]))
        pl.when(jnp.logical_not(side_sends[1 - s]))(
            lambda s=s: clear(ext.at[mid_z, mid_y, pl.ds((cols + CS) * s, CS)]))
        pl.when(jnp.logical_not(row_sends[1 - s]))(
            lambda s=s: clear(ext.at[mid_z, pl.ds((rows + RS) * s, RS), mid_x]))
    fill_bands(dcol, drow)
    pl.semaphore_wait(barrier, peers)

    def first(j, _):
        start_halos(j)
        return 0

    for s in range(2):
        pl.when(side_sends[s])(lambda s=s: side_copy(s).start())
    lax.fori_loop(0, min(AHEAD, chunks), first, 0)
    own.wait()
    for s in range(2):
        pl.when(row_sends[s])(lambda s=s: send_row(s))
    for copy in fetches:
        copy.wait()
    fill_tables(tab, layers * n, cen, wid, col, opa)

    lanes = cols // 128

    def near_copy(p, g):
        at = lax.div(p, 4)
        return pltpu.make_async_remote_copy(
            src_ref=nearbuf.at[g - 1, at],
            dst_ref=neargot.at[g - 1, at],
            send_sem=near_send.at[g - 1, at],
            recv_sem=near_recv.at[g - 1, at],
            device_id={"depth": member(g)},
            device_id_type=MESH,
        )

    def slot(p, k):
        return n // 4 - n // 2**k + lax.div(p, 2 ** (k + 1))

    def far_copy(p, k):
        at = slot(p, k)
        return pltpu.make_async_remote_copy(
            src_ref=farbuf.at[at],
            dst_ref=fargot.at[at],
            send_sem=far_send.at[at],
            recv_sem=far_recv.at[at],
            device_id={"depth": partner(k)},
            device_id_type=MESH,
        )

    def each_tile(body):
        def tile(t, _):
            body(pl.ds(pl.multiple_of(t * 128, 128), 128))
            return 0

        lax.fori_loop(0, lanes, tile, 0)

    def rows_of(p):
        return pl.ds(pl.multiple_of(p * piece, piece), piece)

    def over(a, b):
        return [a[c] + a[3] * b[c] for c in range(3)] + [a[3] * b[3]]

    def coded(ref, here, v):
        for ch in range(4):
            ref[ch, :, here] = encode(1.0 - v[3] if ch == 3 else v[ch])

    def decoded(ref, here):
        v = [decode(ref[ch, :, here]) for ch in range(4)]
        return v[:3] + [1.0 - v[3]]

    def join(k, held, got):
        behind = bit(me, k) == 1
        a = [jnp.where(behind, g, m) for g, m in zip(got, held)]
        b = [jnp.where(behind, m, g) for g, m in zip(got, held)]
        return over(a, b)

    def own_part(p, here):
        return [part[ch, rows_of(p), here] for ch in range(4)]

    def grouped(p, here):
        near = [decoded(neargot.at[g, lax.div(p, 4)], here) for g in range(3)]
        return join(1, join(0, own_part(p, here), near[0]), join(0, near[1], near[2]))

    def joined(v, p, k, here):
        for done in range(2, k):
            v = join(done, v, decoded(fargot.at[slot(p, done)], here))
        return v

    def gathered(p, k):
        for done in range(2, k):
            far_copy(p, done).wait_recv()

    def gather_near(p):
        for g in range(1, 4):
            near_copy(p, g).wait_recv()

    def near_send_piece(p, g):
        each_tile(lambda here: coded(nearbuf.at[g - 1, lax.div(p, 4)], here, own_part(p, here)))
        near_copy(p, g).start()

    def far_send_piece(p, k):
        gather_near(p)
        gathered(p, k)
        each_tile(lambda here: coded(farbuf.at[slot(p, k)], here, joined(grouped(p, here), p, k, here)))
        far_copy(p, k).start()

    def group_own():
        gather_near(me)

        def body(here):
            v = grouped(me, here)
            for ch in range(4):
                part[ch, rows_of(me), here] = v[ch]

        each_tile(body)

    def finish_own():
        gathered(me, rounds)

        def body(here):
            v = joined(own_part(me, here), me, rounds, here)
            for ch in range(4):
                out[ch, 0, :, here] = 1.0 - v[3] if ch == 3 else v[ch] * total(col, ch)[:1]

        each_tile(body)

    for s in range(2):
        pl.when(side_sends[1 - s])(lambda s=s: side_copy(s).wait_recv())

    def slope(i, _):
        at = lax.rem(i + 1, rows // SH)
        for s in range(2):
            edge = at == (rows // SH - 1) * s
            pl.when(jnp.logical_and(row_sends[1 - s], edge))(lambda s=s: place_row(s))
        slopes(pl.multiple_of(at * SH, SH), ext, flat, dcol, drow)
        return 0

    lax.fori_loop(0, rows // SH, slope, 0)

    def chunk(j, _):
        p = order(j)
        pl.when(j + AHEAD < chunks)(lambda: start_halos(j + AHEAD))
        for s in range(2):
            pl.when(sends[1 - s])(lambda s=s: depth_copy(s, p, j).wait_recv())
        march(pl.multiple_of(p * CH, CH), ext, flat, tab, part)
        if early:
            for g in range(1, 4):
                turns = [i for i, turn in enumerate(TURN) if turn % 4 == g]
                pl.when(functools.reduce(jnp.logical_or, [j == i for i in turns]))(lambda g=g: near_send_piece(p, g))
            pl.when(j == GIVE)(lambda: far_send_piece(me + 4 - 8 * bit(me, 2), 2))
        return 0

    lax.fori_loop(0, chunks, chunk, 0)

    if not early:
        for g in range(1, 4):

            def near(h, _, g=g):
                near_send_piece(lax.rem(member(g), 4) + h * 4, g)
                return 0

            lax.fori_loop(0, n // 4, near, 0)
        for k in range(2, rounds):

            def far(h, _, k=k):
                far_send_piece(lax.rem(me, 2**k) + (1 - bit(me, k)) * 2**k + h * 2 ** (k + 1), k)
                return 0

            lax.fori_loop(0, n // 2 ** (k + 1), far, 0)
    def finish(j, _):
        for s in range(2):
            pl.when(sends[s])(lambda s=s: depth_copy(s, j, j).wait_send())
        return 0

    lax.fori_loop(0, chunks, finish, 0)
    for s in range(2):
        pl.when(side_sends[s])(lambda s=s: side_copy(s).wait_send())
    for s in range(2):
        pl.when(row_sends[s])(lambda s=s: row_copy(s).wait_send())

    group_own()
    def near_sent(h, _):
        for g in range(1, 4):
            near_copy(h * 4, g).wait_send()
        return 0

    lax.fori_loop(0, n // 4, near_sent, 0)
    for k in range(2, rounds):

        def far_sent(h, _, k=k):
            far_copy(h * 2 ** (k + 1), k).wait_send()
            return 0

        lax.fori_loop(0, n // 2 ** (k + 1), far_sent, 0)
    finish_own()


def local(volume, cen, wid, col, opa):
    n, ny, nx = lax.axis_size("depth"), lax.axis_size("imgy"), lax.axis_size("imgx")
    layers, rows, cols = volume.shape
    piece = rows // n
    dma = pltpu.SemaphoreType.DMA
    return pl.pallas_call(
        functools.partial(kernel, n, ny, nx),
        out_shape=pltpu.VMEM((4, 1, piece, cols), jnp.float32),
        in_specs=[pl.BlockSpec(memory_space=pltpu.HBM)] * 5,
        out_specs=pl.BlockSpec(memory_space=pltpu.VMEM),
        scratch_shapes=[
            *(pltpu.SMEM(a.shape, jnp.float32) for a in (cen, wid, col, opa)),
            pltpu.VMEM((layers + 2, rows + 2 * RS, cols + 2 * CS), jnp.bfloat16),
            pltpu.VMEM((4, rows, cols), jnp.float32),
            pltpu.VMEM((layers, rows, cols), jnp.float32),
            pltpu.VMEM((512, 256), jnp.bfloat16),
            pltpu.VMEM((SH, SH + 2 * RS), jnp.bfloat16),
            pltpu.VMEM((24, 8, 128), jnp.float32),
            pltpu.VMEM((2, layers, cols), jnp.bfloat16),
            pltpu.VMEM((2, layers, cols), jnp.bfloat16),
            pltpu.VMEM((3, n // 4, 4, piece, cols), jnp.bfloat16),
            pltpu.VMEM((3, n // 4, 4, piece, cols), jnp.bfloat16),
            pltpu.VMEM((n // 4 - 1, 4, piece, cols), jnp.bfloat16),
            pltpu.VMEM((n // 4 - 1, 4, piece, cols), jnp.bfloat16),
            dma,
            dma((4,)),
            dma((2, rows // CH)),
            dma((2, rows // CH)),
            dma((2,)),
            dma((2,)),
            dma((2,)),
            dma((2,)),
            dma((3, n // 4)),
            dma((3, n // 4)),
            dma((n // 4 - 1,)),
            dma((n // 4 - 1,)),
        ],
        compiler_params=pltpu.CompilerParams(
            vmem_limit_bytes=63 * 2**20, collective_id=0, has_side_effects=True
        ),
        name="march_swap",
    )(volume, cen, wid, col, opa)


def solution(mesh):
    return jax.shard_map(
        local,
        mesh=mesh,
        in_specs=(P("depth", "imgy", "imgx"), P(), P(), P(), P()),
        out_specs=P(None, "imgy", "depth", "imgx"),
        check_vma=False,
    )
```

```python
import functools
import math

import jax
import jax.numpy as jnp
from jax import lax
from jax.experimental import pallas as pl
from jax.experimental.pallas import tpu as pltpu
from jax.sharding import PartitionSpec as P

LOG2E = math.log2(math.e)
RS = 16
CS = 128
CH = 32
AHEAD = 8
TURN = (7, 6, 5, 2, 4, 3, 1, 0)
GIVE = 5
SH = 128
MU = 4096.0
POWER = 240.0 / math.log2(1.0 + MU)
MESH = pl.DeviceIdType.MESH


def encode(v):
    return jnp.exp2(jnp.log2(1.0 + MU * v) * POWER - 120.0).astype(jnp.bfloat16)


def decode(y):
    return jnp.exp2((jnp.log2(y.astype(jnp.float32)) + 120.0) * (1.0 / POWER)) * (1.0 / MU) - (1.0 / MU)


def fill_bands(dcol, drow):
    k = lax.broadcasted_iota(jnp.int32, dcol.shape, 0)
    j = lax.broadcasted_iota(jnp.int32, dcol.shape, 1)
    dcol[...] = jnp.where(k == j + CS + 1, 1.0, jnp.where(k == j + CS - 1, -1.0, 0.0)).astype(dcol.dtype)
    i = lax.broadcasted_iota(jnp.int32, drow.shape, 0)
    k = lax.broadcasted_iota(jnp.int32, drow.shape, 1)
    drow[...] = jnp.where(k == i + RS + 1, 1.0, jnp.where(k == i + RS - 1, -1.0, 0.0)).astype(drow.dtype)


def total(colors, c):
    t = jnp.full((8, 128), colors[c, 0], jnp.float32)
    for k in range(1, 4):
        t = t + colors[c, k]
    return t


def fill_tables(tab, layers_all, centers, widths, colors, opacity):
    scale = 1.5 / layers_all * LOG2E
    for k in range(4):
        w = jnp.full((8, 128), widths[k], jnp.float32)
        o = jnp.full((8, 128), opacity[k], jnp.float32) * scale
        tab[k] = jnp.full((8, 128), centers[k], jnp.float32)
        tab[4 + k] = -LOG2E / (w * w)
        tab[8 + k] = jnp.log2(o)
        for c in range(3):
            tab[12 + 4 * c + k] = 0.7 * colors[c, k] / o / total(colors, c)


def slopes(r0, ext, flat, dcol, drow):
    layers, cols = ext.shape[0] - 2, ext.shape[2] - 2 * CS
    here = pl.ds(r0, SH)
    for z in range(layers):
        r = jnp.dot(
            drow[...], ext[1 + z, pl.ds(r0, SH + 2 * RS), CS : CS + cols], preferred_element_type=jnp.float32
        )
        flat[z, here, :] = r * r + 1.0
    for h in range(cols // 256):
        at = slice(h * 256, h * 256 + 256)
        left = ext[1 : layers + 1, pl.ds(r0 + RS, SH), h * 256 : h * 256 + 512].reshape(layers * SH, 512)
        c = jnp.dot(left, dcol[...], preferred_element_type=jnp.float32).reshape(layers, SH, 256)
        flat[:, here, at] = flat[:, here, at] + c * c


def table(tab, i):
    return jnp.concatenate([tab[i], tab[i]], axis=0)


def bumps_of(s, cen, quad, off):
    bump = []
    for k in range(4):
        u = s - cen[k]
        bump.append(jnp.exp2(u * u * quad[k] + off[k]))
    return bump, (bump[0] + bump[1]) + (bump[2] + bump[3])


def tinted(tab, ch, acc):
    m = [table(tab, 12 + 4 * ch + k) for k in range(4)]
    return (m[0] * acc[0] + m[1] * acc[1]) + (m[2] * acc[2] + m[3] * acc[3])


def march(r0, ext, flat, tab, part):
    layers, cols = ext.shape[0] - 2, ext.shape[2] - 2 * CS
    tiles = cols // 128

    def tile(t, _):
        q0 = pl.multiple_of(r0 + t // tiles * 16, 16)
        l0 = pl.multiple_of(t % tiles * 128, 128)
        rows, lanes = pl.ds(q0, 16), pl.ds(l0, 128)

        def plane(z):
            return ext[z, pl.ds(pl.multiple_of(q0 + RS, 16), 16), pl.ds(l0 + CS, 128)].astype(jnp.float32)

        cen, quad, off = [[table(tab, 4 * i + k) for k in range(4)] for i in range(3)]
        acc = [jnp.zeros((16, 128), jnp.float32) for _ in range(4)]
        expo = jnp.zeros((16, 128), jnp.float32)
        passed = jnp.ones((16, 128), jnp.float32)
        before, s = plane(0), plane(1)
        for z in range(layers):
            after = plane(z + 2)
            d = after - before
            light = jnp.abs(d) * lax.rsqrt(d * d + flat[z, rows, lanes]) + (0.3 / 0.7)
            bump, thick = bumps_of(s, cen, quad, off)
            expo = expo - thick
            later = jnp.exp2(expo)
            weight = (passed - later) * light
            for k in range(4):
                acc[k] = acc[k] + weight * bump[k]
            passed = later
            before, s = s, after
        for ch in range(3):
            part[ch, rows, lanes] = tinted(tab, ch, acc)
        part[3, rows, lanes] = passed
        return 0

    lax.fori_loop(0, CH // 16 * tiles, tile, 0, unroll=2)


def kernel(n, ny, nx, vol, cen_h, wid_h, col_h, opa_h, out, cen, wid, col, opa,
           ext, part, flat, dcol, drow, tab, rowbuf, rowgot, nearbuf, neargot, farbuf, fargot,
           local_sem, fetch_sem, depth_send, depth_recv, side_send, side_recv, row_send, row_recv,
           near_send, near_recv, far_send, far_recv):
    layers, rows, cols = vol.shape
    me, iy, ix = lax.axis_index("depth"), lax.axis_index("imgy"), lax.axis_index("imgx")
    piece = rows // n
    chunks = rows // CH
    rounds = n.bit_length() - 1
    early = piece == CH and n == len(TURN)

    mid_z, mid_y, mid_x = pl.ds(1, layers), pl.ds(RS, rows), pl.ds(CS, cols)
    fetches = [pltpu.make_async_copy(a, b, fetch_sem.at[i]) for i, (a, b) in enumerate(
        ((cen_h, cen), (wid_h, wid), (col_h, col), (opa_h, opa)))]
    own = pltpu.make_async_copy(vol, ext.at[mid_z, mid_y, mid_x], local_sem)

    def bit(dev, k):
        return lax.rem(lax.div(dev, 2**k), 2)

    def partner(k):
        return me + (1 - 2 * bit(me, k)) * 2**k

    def member(g):
        return me + sum((1 - 2 * bit(me, k)) * 2**k for k in range(2) if g >> k & 1)

    def away(dev, flips, mask):
        return dev + sum(flips[k] * bit(mask, k) for k in range(rounds))

    def order_of(dev):
        flips = [(1 - 2 * bit(dev, k)) * 2**k for k in range(rounds)]

        def order(j):
            if not early:
                return j
            mask = sum((j == i).astype(jnp.int32) * turn for i, turn in enumerate(TURN))
            return away(dev, flips, mask)

        return order

    order = order_of(me)
    order_there = [order_of(me + 1), order_of(me - 1)]

    barrier = pltpu.get_barrier_semaphore()

    def greet(dev):
        pl.semaphore_signal(barrier, inc=1, device_id=dev, device_id_type=MESH)

    for g in range(1, 4):
        greet({"depth": member(g)})
    for k in range(2, rounds):
        greet({"depth": partner(k)})
    peers = jnp.int32(rounds + 1)
    other = me + 2 * bit(me, 0) - 1
    for name, at, there in (
        ("depth", other, jnp.logical_and(other >= 0, other < n)),
        ("imgy", iy - 1, iy > 0),
        ("imgy", iy + 1, iy < ny - 1),
        ("imgx", ix - 1, ix > 0),
        ("imgx", ix + 1, ix < nx - 1),
    ):
        pl.when(there)(lambda name=name, at=at: greet({name: at}))
        peers = peers + there.astype(jnp.int32)
    own.start()
    for copy in fetches:
        copy.start()

    def depth_copy(side, p, j):
        r0 = pl.multiple_of(p * CH, CH)
        return pltpu.make_async_remote_copy(
            src_ref=vol.at[pl.ds((layers - 1) * (1 - side), 1), pl.ds(r0, CH), :],
            dst_ref=ext.at[pl.ds((layers + 1) * side, 1), pl.ds(r0 + RS, CH), mid_x],
            send_sem=depth_send.at[side, j],
            recv_sem=depth_recv.at[side, j],
            device_id={"depth": me + 1 - 2 * side},
            device_id_type=MESH,
        )

    def side_copy(side):
        return pltpu.make_async_remote_copy(
            src_ref=vol.at[:, :, pl.ds((cols - CS) * (1 - side), CS)],
            dst_ref=ext.at[mid_z, mid_y, pl.ds((cols + CS) * side, CS)],
            send_sem=side_send.at[side],
            recv_sem=side_recv.at[side],
            device_id={"imgx": ix + 1 - 2 * side},
            device_id_type=MESH,
        )

    def row_copy(side):
        return pltpu.make_async_remote_copy(
            src_ref=rowbuf.at[side],
            dst_ref=rowgot.at[side],
            send_sem=row_send.at[side],
            recv_sem=row_recv.at[side],
            device_id={"imgy": iy + 1 - 2 * side},
            device_id_type=MESH,
        )

    def send_row(side):
        at, pick = (rows, RS - 1) if side == 0 else (RS, 0)
        edge = [ext[1 + z, at : at + RS, mid_x].astype(jnp.float32)[pick : pick + 1] for z in range(layers)]
        rowbuf[side] = jnp.concatenate(edge, axis=0).astype(jnp.bfloat16)
        row_copy(side).start()

    def place_row(side):
        row_copy(side).wait_recv()
        got = rowgot[side].astype(jnp.float32)
        at = (rows + RS) * side
        for z in range(layers):
            ext[1 + z, at : at + RS, mid_x] = jnp.broadcast_to(got[z : z + 1], (RS, cols)).astype(jnp.bfloat16)

    sends = (me < n - 1, me > 0)
    side_sends = (ix < nx - 1, ix > 0)
    row_sends = (iy < ny - 1, iy > 0)

    def start_halos(j):
        for s in range(2):
            pl.when(sends[s])(lambda s=s: depth_copy(s, order_there[s](j), j).start())

    def clear(region):
        region[...] = jnp.zeros(region.shape, region.dtype)

    for s in range(2):
        pl.when(jnp.logical_not(sends[1 - s]))(lambda s=s: clear(ext.at[pl.ds((layers + 1) * s, 1), mid_y, mid_x]))
        pl.when(jnp.logical_not(side_sends[1 - s]))(
            lambda s=s: clear(ext.at[mid_z, mid_y, pl.ds((cols + CS) * s, CS)]))
        pl.when(jnp.logical_not(row_sends[1 - s]))(
            lambda s=s: clear(ext.at[mid_z, pl.ds((rows + RS) * s, RS), mid_x]))
    fill_bands(dcol, drow)
    pl.semaphore_wait(barrier, peers)

    def first(j, _):
        start_halos(j)
        return 0

    for s in range(2):
        pl.when(side_sends[s])(lambda s=s: side_copy(s).start())
    lax.fori_loop(0, min(AHEAD, chunks), first, 0)
    own.wait()
    for s in range(2):
        pl.when(row_sends[s])(lambda s=s: send_row(s))
    for copy in fetches:
        copy.wait()
    fill_tables(tab, layers * n, cen, wid, col, opa)

    lanes = cols // 128

    def near_copy(p, g):
        at = lax.div(p, 4)
        return pltpu.make_async_remote_copy(
            src_ref=nearbuf.at[g - 1, at],
            dst_ref=neargot.at[g - 1, at],
            send_sem=near_send.at[g - 1, at],
            recv_sem=near_recv.at[g - 1, at],
            device_id={"depth": member(g)},
            device_id_type=MESH,
        )

    def slot(p, k):
        return n // 4 - n // 2**k + lax.div(p, 2 ** (k + 1))

    def far_copy(p, k):
        at = slot(p, k)
        return pltpu.make_async_remote_copy(
            src_ref=farbuf.at[at],
            dst_ref=fargot.at[at],
            send_sem=far_send.at[at],
            recv_sem=far_recv.at[at],
            device_id={"depth": partner(k)},
            device_id_type=MESH,
        )

    def each_tile(body):
        def tile(t, _):
            body(pl.ds(pl.multiple_of(t * 128, 128), 128))
            return 0

        lax.fori_loop(0, lanes, tile, 0)

    def rows_of(p):
        return pl.ds(pl.multiple_of(p * piece, piece), piece)

    def over(a, b):
        return [a[c] + a[3] * b[c] for c in range(3)] + [a[3] * b[3]]

    def coded(ref, here, v):
        for ch in range(4):
            ref[ch, :, here] = encode(1.0 - v[3] if ch == 3 else v[ch])

    def decoded(ref, here):
        v = [decode(ref[ch, :, here]) for ch in range(4)]
        return v[:3] + [1.0 - v[3]]

    def join(k, held, got):
        behind = bit(me, k) == 1
        a = [jnp.where(behind, g, m) for g, m in zip(got, held)]
        b = [jnp.where(behind, m, g) for g, m in zip(got, held)]
        return over(a, b)

    def own_part(p, here):
        return [part[ch, rows_of(p), here] for ch in range(4)]

    def grouped(p, here):
        near = [decoded(neargot.at[g, lax.div(p, 4)], here) for g in range(3)]
        return join(1, join(0, own_part(p, here), near[0]), join(0, near[1], near[2]))

    def joined(v, p, k, here):
        for done in range(2, k):
            v = join(done, v, decoded(fargot.at[slot(p, done)], here))
        return v

    def gathered(p, k):
        for done in range(2, k):
            far_copy(p, done).wait_recv()

    def gather_near(p):
        for g in range(1, 4):
            near_copy(p, g).wait_recv()

    def near_send_piece(p, g):
        each_tile(lambda here: coded(nearbuf.at[g - 1, lax.div(p, 4)], here, own_part(p, here)))
        near_copy(p, g).start()

    def far_send_piece(p, k):
        gather_near(p)
        gathered(p, k)
        each_tile(lambda here: coded(farbuf.at[slot(p, k)], here, joined(grouped(p, here), p, k, here)))
        far_copy(p, k).start()

    def group_own():
        gather_near(me)

        def body(here):
            v = grouped(me, here)
            for ch in range(4):
                part[ch, rows_of(me), here] = v[ch]

        each_tile(body)

    def finish_own():
        gathered(me, rounds)

        def body(here):
            v = joined(own_part(me, here), me, rounds, here)
            for ch in range(4):
                out[ch, 0, :, here] = 1.0 - v[3] if ch == 3 else v[ch] * total(col, ch)[:1]

        each_tile(body)

    for s in range(2):
        pl.when(side_sends[1 - s])(lambda s=s: side_copy(s).wait_recv())

    def slope(i, _):
        at = lax.rem(i + 1, rows // SH)
        for s in range(2):
            edge = at == (rows // SH - 1) * s
            pl.when(jnp.logical_and(row_sends[1 - s], edge))(lambda s=s: place_row(s))
        slopes(pl.multiple_of(at * SH, SH), ext, flat, dcol, drow)
        return 0

    lax.fori_loop(0, rows // SH, slope, 0)

    def chunk(j, _):
        p = order(j)
        pl.when(j + AHEAD < chunks)(lambda: start_halos(j + AHEAD))
        for s in range(2):
            pl.when(sends[1 - s])(lambda s=s: depth_copy(s, p, j).wait_recv())
        march(pl.multiple_of(p * CH, CH), ext, flat, tab, part)
        if early:
            for g in range(1, 4):
                turns = [i for i, turn in enumerate(TURN) if turn % 4 == g]
                pl.when(functools.reduce(jnp.logical_or, [j == i for i in turns]))(lambda g=g: near_send_piece(p, g))
            pl.when(j == GIVE)(lambda: far_send_piece(me + 4 - 8 * bit(me, 2), 2))
        return 0

    lax.fori_loop(0, chunks, chunk, 0)

    if not early:
        for g in range(1, 4):

            def near(h, _, g=g):
                near_send_piece(lax.rem(member(g), 4) + h * 4, g)
                return 0

            lax.fori_loop(0, n // 4, near, 0)
        for k in range(2, rounds):

            def far(h, _, k=k):
                far_send_piece(lax.rem(me, 2**k) + (1 - bit(me, k)) * 2**k + h * 2 ** (k + 1), k)
                return 0

            lax.fori_loop(0, n // 2 ** (k + 1), far, 0)
    def finish(j, _):
        for s in range(2):
            pl.when(sends[s])(lambda s=s: depth_copy(s, j, j).wait_send())
        return 0

    lax.fori_loop(0, chunks, finish, 0)
    for s in range(2):
        pl.when(side_sends[s])(lambda s=s: side_copy(s).wait_send())
    for s in range(2):
        pl.when(row_sends[s])(lambda s=s: row_copy(s).wait_send())

    group_own()
    def near_sent(h, _):
        for g in range(1, 4):
            near_copy(h * 4, g).wait_send()
        return 0

    lax.fori_loop(0, n // 4, near_sent, 0)
    for k in range(2, rounds):

        def far_sent(h, _, k=k):
            far_copy(h * 2 ** (k + 1), k).wait_send()
            return 0

        lax.fori_loop(0, n // 2 ** (k + 1), far_sent, 0)
    finish_own()


def local(volume, cen, wid, col, opa):
    n, ny, nx = lax.axis_size("depth"), lax.axis_size("imgy"), lax.axis_size("imgx")
    layers, rows, cols = volume.shape
    piece = rows // n
    dma = pltpu.SemaphoreType.DMA
    return pl.pallas_call(
        functools.partial(kernel, n, ny, nx),
        out_shape=pltpu.VMEM((4, 1, piece, cols), jnp.float32),
        in_specs=[pl.BlockSpec(memory_space=pltpu.HBM)] * 5,
        out_specs=pl.BlockSpec(memory_space=pltpu.VMEM),
        scratch_shapes=[
            *(pltpu.SMEM(a.shape, jnp.float32) for a in (cen, wid, col, opa)),
            pltpu.VMEM((layers + 2, rows + 2 * RS, cols + 2 * CS), jnp.bfloat16),
            pltpu.VMEM((4, rows, cols), jnp.float32),
            pltpu.VMEM((layers, rows, cols), jnp.float32),
            pltpu.VMEM((512, 256), jnp.bfloat16),
            pltpu.VMEM((SH, SH + 2 * RS), jnp.bfloat16),
            pltpu.VMEM((24, 8, 128), jnp.float32),
            pltpu.VMEM((2, layers, cols), jnp.bfloat16),
            pltpu.VMEM((2, layers, cols), jnp.bfloat16),
            pltpu.VMEM((3, n // 4, 4, piece, cols), jnp.bfloat16),
            pltpu.VMEM((3, n // 4, 4, piece, cols), jnp.bfloat16),
            pltpu.VMEM((n // 4 - 1, 4, piece, cols), jnp.bfloat16),
            pltpu.VMEM((n // 4 - 1, 4, piece, cols), jnp.bfloat16),
            dma,
            dma((4,)),
            dma((2, rows // CH)),
            dma((2, rows // CH)),
            dma((2,)),
            dma((2,)),
            dma((2,)),
            dma((2,)),
            dma((3, n // 4)),
            dma((3, n // 4)),
            dma((n // 4 - 1,)),
            dma((n // 4 - 1,)),
        ],
        compiler_params=pltpu.CompilerParams(
            vmem_limit_bytes=63 * 2**20, collective_id=0, has_side_effects=True
        ),
        name="march_swap",
    )(volume, cen, wid, col, opa)


def solution(mesh):
    return jax.shard_map(
        local,
        mesh=mesh,
        in_specs=(P("depth", "imgy", "imgx"), P(), P(), P(), P()),
        out_specs=P(None, "imgy", "depth", "imgx"),
        check_vma=False,
    )
```

```python
import functools
import math

import jax
import jax.numpy as jnp
from jax import lax
from jax.experimental import pallas as pl
from jax.experimental.pallas import tpu as pltpu
from jax.sharding import PartitionSpec as P

LOG2E = math.log2(math.e)
RS = 16
CS = 128
CH = 32
AHEAD = 8
TURN = (7, 6, 5, 2, 4, 3, 1, 0)
GIVE = 5
SH = 128
MU = 4096.0
POWER = 240.0 / math.log2(1.0 + MU)
MESH = pl.DeviceIdType.MESH


def encode(v):
    return jnp.exp2(jnp.log2(1.0 + MU * v) * POWER - 120.0).astype(jnp.bfloat16)


def decode(y):
    return jnp.exp2((jnp.log2(y.astype(jnp.float32)) + 120.0) * (1.0 / POWER)) * (1.0 / MU) - (1.0 / MU)


def fill_bands(dcol, drow):
    k = lax.broadcasted_iota(jnp.int32, dcol.shape, 0)
    j = lax.broadcasted_iota(jnp.int32, dcol.shape, 1)
    dcol[...] = jnp.where(k == j + CS + 1, 1.0, jnp.where(k == j + CS - 1, -1.0, 0.0)).astype(dcol.dtype)
    i = lax.broadcasted_iota(jnp.int32, drow.shape, 0)
    k = lax.broadcasted_iota(jnp.int32, drow.shape, 1)
    drow[...] = jnp.where(k == i + RS + 1, 1.0, jnp.where(k == i + RS - 1, -1.0, 0.0)).astype(drow.dtype)


def total(colors, c):
    t = jnp.full((8, 128), colors[c, 0], jnp.float32)
    for k in range(1, 4):
        t = t + colors[c, k]
    return t


def fill_tables(tab, layers_all, centers, widths, colors, opacity):
    scale = 1.5 / layers_all * LOG2E
    for k in range(4):
        w = jnp.full((8, 128), widths[k], jnp.float32)
        o = jnp.full((8, 128), opacity[k], jnp.float32) * scale
        tab[k] = jnp.full((8, 128), centers[k], jnp.float32)
        tab[4 + k] = -LOG2E / (w * w)
        tab[8 + k] = jnp.log2(o)
        for c in range(3):
            tab[12 + 4 * c + k] = 0.7 * colors[c, k] / o / total(colors, c)


def slopes(r0, ext, flat, dcol, drow):
    layers, cols = ext.shape[0] - 2, ext.shape[2] - 2 * CS
    here = pl.ds(r0, SH)
    for z in range(layers):
        r = jnp.dot(
            drow[...], ext[1 + z, pl.ds(r0, SH + 2 * RS), CS : CS + cols], preferred_element_type=jnp.float32
        )
        flat[z, here, :] = r * r + 1.0
    for h in range(cols // 256):
        at = slice(h * 256, h * 256 + 256)
        left = ext[1 : layers + 1, pl.ds(r0 + RS, SH), h * 256 : h * 256 + 512].reshape(layers * SH, 512)
        c = jnp.dot(left, dcol[...], preferred_element_type=jnp.float32).reshape(layers, SH, 256)
        flat[:, here, at] = flat[:, here, at] + c * c


def table(tab, i):
    return jnp.concatenate([tab[i], tab[i]], axis=0)


def bumps_of(s, cen, quad, off):
    bump = []
    for k in range(4):
        u = s - cen[k]
        bump.append(jnp.exp2(u * u * quad[k] + off[k]))
    return bump, (bump[0] + bump[1]) + (bump[2] + bump[3])


def tinted(tab, ch, acc):
    m = [table(tab, 12 + 4 * ch + k) for k in range(4)]
    return (m[0] * acc[0] + m[1] * acc[1]) + (m[2] * acc[2] + m[3] * acc[3])


def march(r0, ext, flat, tab, part):
    layers, cols = ext.shape[0] - 2, ext.shape[2] - 2 * CS
    tiles = cols // 128

    def tile(t, _):
        q0 = pl.multiple_of(r0 + t // tiles * 16, 16)
        l0 = pl.multiple_of(t % tiles * 128, 128)
        rows, lanes = pl.ds(q0, 16), pl.ds(l0, 128)

        def plane(z):
            return ext[z, pl.ds(pl.multiple_of(q0 + RS, 16), 16), pl.ds(l0 + CS, 128)].astype(jnp.float32)

        cen, quad, off = [[table(tab, 4 * i + k) for k in range(4)] for i in range(3)]
        acc = [jnp.zeros((16, 128), jnp.float32) for _ in range(4)]
        expo = jnp.zeros((16, 128), jnp.float32)
        passed = jnp.ones((16, 128), jnp.float32)
        before, s = plane(0), plane(1)
        for z in range(layers):
            after = plane(z + 2)
            d = after - before
            light = jnp.abs(d) * lax.rsqrt(d * d + flat[z, rows, lanes]) + (0.3 / 0.7)
            bump, thick = bumps_of(s, cen, quad, off)
            expo = expo - thick
            later = jnp.exp2(expo)
            weight = (passed - later) * light
            for k in range(4):
                acc[k] = acc[k] + weight * bump[k]
            passed = later
            before, s = s, after
        for ch in range(3):
            part[ch, rows, lanes] = tinted(tab, ch, acc)
        part[3, rows, lanes] = passed
        return 0

    lax.fori_loop(0, CH // 16 * tiles, tile, 0, unroll=2)


def kernel(n, ny, nx, vol, cen_h, wid_h, col_h, opa_h, out, cen, wid, col, opa,
           ext, part, flat, dcol, drow, tab, rowbuf, rowgot, nearbuf, neargot, farbuf, fargot,
           local_sem, fetch_sem, depth_send, depth_recv, side_send, side_recv, row_send, row_recv,
           near_send, near_recv, far_send, far_recv):
    layers, rows, cols = vol.shape
    me, iy, ix = lax.axis_index("depth"), lax.axis_index("imgy"), lax.axis_index("imgx")
    piece = rows // n
    chunks = rows // CH
    rounds = n.bit_length() - 1
    early = piece == CH and n == len(TURN)

    mid_z, mid_y, mid_x = pl.ds(1, layers), pl.ds(RS, rows), pl.ds(CS, cols)
    fetches = [pltpu.make_async_copy(a, b, fetch_sem.at[i]) for i, (a, b) in enumerate(
        ((cen_h, cen), (wid_h, wid), (col_h, col), (opa_h, opa)))]
    own = pltpu.make_async_copy(vol, ext.at[mid_z, mid_y, mid_x], local_sem)

    def bit(dev, k):
        return lax.rem(lax.div(dev, 2**k), 2)

    def partner(k):
        return me + (1 - 2 * bit(me, k)) * 2**k

    def member(g):
        return me + sum((1 - 2 * bit(me, k)) * 2**k for k in range(2) if g >> k & 1)

    def away(dev, flips, mask):
        return dev + sum(flips[k] * bit(mask, k) for k in range(rounds))

    def order_of(dev):
        flips = [(1 - 2 * bit(dev, k)) * 2**k for k in range(rounds)]

        def order(j):
            if not early:
                return j
            mask = sum((j == i).astype(jnp.int32) * turn for i, turn in enumerate(TURN))
            return away(dev, flips, mask)

        return order

    order = order_of(me)
    order_there = [order_of(me + 1), order_of(me - 1)]

    barrier = pltpu.get_barrier_semaphore()

    def greet(dev):
        pl.semaphore_signal(barrier, inc=1, device_id=dev, device_id_type=MESH)

    for g in range(1, 4):
        greet({"depth": member(g)})
    for k in range(2, rounds):
        greet({"depth": partner(k)})
    peers = jnp.int32(rounds + 1)
    other = me + 2 * bit(me, 0) - 1
    for name, at, there in (
        ("depth", other, jnp.logical_and(other >= 0, other < n)),
        ("imgy", iy - 1, iy > 0),
        ("imgy", iy + 1, iy < ny - 1),
        ("imgx", ix - 1, ix > 0),
        ("imgx", ix + 1, ix < nx - 1),
    ):
        pl.when(there)(lambda name=name, at=at: greet({name: at}))
        peers = peers + there.astype(jnp.int32)
    own.start()
    for copy in fetches:
        copy.start()

    def depth_copy(side, p, j):
        r0 = pl.multiple_of(p * CH, CH)
        return pltpu.make_async_remote_copy(
            src_ref=vol.at[pl.ds((layers - 1) * (1 - side), 1), pl.ds(r0, CH), :],
            dst_ref=ext.at[pl.ds((layers + 1) * side, 1), pl.ds(r0 + RS, CH), mid_x],
            send_sem=depth_send.at[side, j],
            recv_sem=depth_recv.at[side, j],
            device_id={"depth": me + 1 - 2 * side},
            device_id_type=MESH,
        )

    def side_copy(side):
        return pltpu.make_async_remote_copy(
            src_ref=vol.at[:, :, pl.ds((cols - CS) * (1 - side), CS)],
            dst_ref=ext.at[mid_z, mid_y, pl.ds((cols + CS) * side, CS)],
            send_sem=side_send.at[side],
            recv_sem=side_recv.at[side],
            device_id={"imgx": ix + 1 - 2 * side},
            device_id_type=MESH,
        )

    def row_copy(side):
        return pltpu.make_async_remote_copy(
            src_ref=rowbuf.at[side],
            dst_ref=rowgot.at[side],
            send_sem=row_send.at[side],
            recv_sem=row_recv.at[side],
            device_id={"imgy": iy + 1 - 2 * side},
            device_id_type=MESH,
        )

    def send_row(side):
        at, pick = (rows, RS - 1) if side == 0 else (RS, 0)
        edge = [ext[1 + z, at : at + RS, mid_x].astype(jnp.float32)[pick : pick + 1] for z in range(layers)]
        rowbuf[side] = jnp.concatenate(edge, axis=0).astype(jnp.bfloat16)
        row_copy(side).start()

    def place_row(side):
        row_copy(side).wait_recv()
        got = rowgot[side].astype(jnp.float32)
        at = (rows + RS) * side
        for z in range(layers):
            ext[1 + z, at : at + RS, mid_x] = jnp.broadcast_to(got[z : z + 1], (RS, cols)).astype(jnp.bfloat16)

    sends = (me < n - 1, me > 0)
    side_sends = (ix < nx - 1, ix > 0)
    row_sends = (iy < ny - 1, iy > 0)

    def start_halos(j):
        for s in range(2):
            pl.when(sends[s])(lambda s=s: depth_copy(s, order_there[s](j), j).start())

    def clear(region):
        region[...] = jnp.zeros(region.shape, region.dtype)

    for s in range(2):
        pl.when(jnp.logical_not(sends[1 - s]))(lambda s=s: clear(ext.at[pl.ds((layers + 1) * s, 1), mid_y, mid_x]))
        pl.when(jnp.logical_not(side_sends[1 - s]))(
            lambda s=s: clear(ext.at[mid_z, mid_y, pl.ds((cols + CS) * s, CS)]))
        pl.when(jnp.logical_not(row_sends[1 - s]))(
            lambda s=s: clear(ext.at[mid_z, pl.ds((rows + RS) * s, RS), mid_x]))
    fill_bands(dcol, drow)
    pl.semaphore_wait(barrier, peers)

    def first(j, _):
        start_halos(j)
        return 0

    lax.fori_loop(0, 2, first, 0)
    for s in range(2):
        pl.when(side_sends[s])(lambda s=s: side_copy(s).start())
    lax.fori_loop(2, min(AHEAD, chunks), first, 0)
    own.wait()
    for s in range(2):
        pl.when(row_sends[s])(lambda s=s: send_row(s))
    for copy in fetches:
        copy.wait()
    fill_tables(tab, layers * n, cen, wid, col, opa)

    lanes = cols // 128

    def near_copy(p, g):
        at = lax.div(p, 4)
        return pltpu.make_async_remote_copy(
            src_ref=nearbuf.at[g - 1, at],
            dst_ref=neargot.at[g - 1, at],
            send_sem=near_send.at[g - 1, at],
            recv_sem=near_recv.at[g - 1, at],
            device_id={"depth": member(g)},
            device_id_type=MESH,
        )

    def slot(p, k):
        return n // 4 - n // 2**k + lax.div(p, 2 ** (k + 1))

    def far_copy(p, k):
        at = slot(p, k)
        return pltpu.make_async_remote_copy(
            src_ref=farbuf.at[at],
            dst_ref=fargot.at[at],
            send_sem=far_send.at[at],
            recv_sem=far_recv.at[at],
            device_id={"depth": partner(k)},
            device_id_type=MESH,
        )

    def each_tile(body):
        def tile(t, _):
            body(pl.ds(pl.multiple_of(t * 128, 128), 128))
            return 0

        lax.fori_loop(0, lanes, tile, 0)

    def rows_of(p):
        return pl.ds(pl.multiple_of(p * piece, piece), piece)

    def over(a, b):
        return [a[c] + a[3] * b[c] for c in range(3)] + [a[3] * b[3]]

    def coded(ref, here, v):
        for ch in range(4):
            ref[ch, :, here] = encode(1.0 - v[3] if ch == 3 else v[ch])

    def decoded(ref, here):
        v = [decode(ref[ch, :, here]) for ch in range(4)]
        return v[:3] + [1.0 - v[3]]

    def join(k, held, got):
        behind = bit(me, k) == 1
        a = [jnp.where(behind, g, m) for g, m in zip(got, held)]
        b = [jnp.where(behind, m, g) for g, m in zip(got, held)]
        return over(a, b)

    def own_part(p, here):
        return [part[ch, rows_of(p), here] for ch in range(4)]

    def grouped(p, here):
        near = [decoded(neargot.at[g, lax.div(p, 4)], here) for g in range(3)]
        return join(1, join(0, own_part(p, here), near[0]), join(0, near[1], near[2]))

    def joined(v, p, k, here):
        for done in range(2, k):
            v = join(done, v, decoded(fargot.at[slot(p, done)], here))
        return v

    def gathered(p, k):
        for done in range(2, k):
            far_copy(p, done).wait_recv()

    def gather_near(p):
        for g in range(1, 4):
            near_copy(p, g).wait_recv()

    def near_send_piece(p, g):
        each_tile(lambda here: coded(nearbuf.at[g - 1, lax.div(p, 4)], here, own_part(p, here)))
        near_copy(p, g).start()

    def far_send_piece(p, k):
        gather_near(p)
        gathered(p, k)
        each_tile(lambda here: coded(farbuf.at[slot(p, k)], here, joined(grouped(p, here), p, k, here)))
        far_copy(p, k).start()

    def group_own():
        gather_near(me)

        def body(here):
            v = grouped(me, here)
            for ch in range(4):
                part[ch, rows_of(me), here] = v[ch]

        each_tile(body)

    def finish_own():
        gathered(me, rounds)

        def body(here):
            v = joined(own_part(me, here), me, rounds, here)
            for ch in range(4):
                out[ch, 0, :, here] = 1.0 - v[3] if ch == 3 else v[ch] * total(col, ch)[:1]

        each_tile(body)

    for s in range(2):
        pl.when(side_sends[1 - s])(lambda s=s: side_copy(s).wait_recv())

    def slope(i, _):
        at = lax.rem(i + 1, rows // SH)
        for s in range(2):
            edge = at == (rows // SH - 1) * s
            pl.when(jnp.logical_and(row_sends[1 - s], edge))(lambda s=s: place_row(s))
        slopes(pl.multiple_of(at * SH, SH), ext, flat, dcol, drow)
        return 0

    lax.fori_loop(0, rows // SH, slope, 0)

    def chunk(j, _):
        p = order(j)
        pl.when(j + AHEAD < chunks)(lambda: start_halos(j + AHEAD))
        for s in range(2):
            pl.when(sends[1 - s])(lambda s=s: depth_copy(s, p, j).wait_recv())
        march(pl.multiple_of(p * CH, CH), ext, flat, tab, part)
        if early:
            for g in range(1, 4):
                turns = [i for i, turn in enumerate(TURN) if turn % 4 == g]
                pl.when(functools.reduce(jnp.logical_or, [j == i for i in turns]))(lambda g=g: near_send_piece(p, g))
            pl.when(j == GIVE)(lambda: far_send_piece(me + 4 - 8 * bit(me, 2), 2))
        return 0

    lax.fori_loop(0, chunks, chunk, 0)

    if not early:
        for g in range(1, 4):

            def near(h, _, g=g):
                near_send_piece(lax.rem(member(g), 4) + h * 4, g)
                return 0

            lax.fori_loop(0, n // 4, near, 0)
        for k in range(2, rounds):

            def far(h, _, k=k):
                far_send_piece(lax.rem(me, 2**k) + (1 - bit(me, k)) * 2**k + h * 2 ** (k + 1), k)
                return 0

            lax.fori_loop(0, n // 2 ** (k + 1), far, 0)
    def finish(j, _):
        for s in range(2):
            pl.when(sends[s])(lambda s=s: depth_copy(s, j, j).wait_send())
        return 0

    lax.fori_loop(0, chunks, finish, 0)
    for s in range(2):
        pl.when(side_sends[s])(lambda s=s: side_copy(s).wait_send())
    for s in range(2):
        pl.when(row_sends[s])(lambda s=s: row_copy(s).wait_send())

    group_own()
    def near_sent(h, _):
        for g in range(1, 4):
            near_copy(h * 4, g).wait_send()
        return 0

    lax.fori_loop(0, n // 4, near_sent, 0)
    for k in range(2, rounds):

        def far_sent(h, _, k=k):
            far_copy(h * 2 ** (k + 1), k).wait_send()
            return 0

        lax.fori_loop(0, n // 2 ** (k + 1), far_sent, 0)
    finish_own()


def local(volume, cen, wid, col, opa):
    n, ny, nx = lax.axis_size("depth"), lax.axis_size("imgy"), lax.axis_size("imgx")
    layers, rows, cols = volume.shape
    piece = rows // n
    dma = pltpu.SemaphoreType.DMA
    return pl.pallas_call(
        functools.partial(kernel, n, ny, nx),
        out_shape=pltpu.VMEM((4, 1, piece, cols), jnp.float32),
        in_specs=[pl.BlockSpec(memory_space=pltpu.HBM)] * 5,
        out_specs=pl.BlockSpec(memory_space=pltpu.VMEM),
        scratch_shapes=[
            *(pltpu.SMEM(a.shape, jnp.float32) for a in (cen, wid, col, opa)),
            pltpu.VMEM((layers + 2, rows + 2 * RS, cols + 2 * CS), jnp.bfloat16),
            pltpu.VMEM((4, rows, cols), jnp.float32),
            pltpu.VMEM((layers, rows, cols), jnp.float32),
            pltpu.VMEM((512, 256), jnp.bfloat16),
            pltpu.VMEM((SH, SH + 2 * RS), jnp.bfloat16),
            pltpu.VMEM((24, 8, 128), jnp.float32),
            pltpu.VMEM((2, layers, cols), jnp.bfloat16),
            pltpu.VMEM((2, layers, cols), jnp.bfloat16),
            pltpu.VMEM((3, n // 4, 4, piece, cols), jnp.bfloat16),
            pltpu.VMEM((3, n // 4, 4, piece, cols), jnp.bfloat16),
            pltpu.VMEM((n // 4 - 1, 4, piece, cols), jnp.bfloat16),
            pltpu.VMEM((n // 4 - 1, 4, piece, cols), jnp.bfloat16),
            dma,
            dma((4,)),
            dma((2, rows // CH)),
            dma((2, rows // CH)),
            dma((2,)),
            dma((2,)),
            dma((2,)),
            dma((2,)),
            dma((3, n // 4)),
            dma((3, n // 4)),
            dma((n // 4 - 1,)),
            dma((n // 4 - 1,)),
        ],
        compiler_params=pltpu.CompilerParams(
            vmem_limit_bytes=63 * 2**20, collective_id=0, has_side_effects=True
        ),
        name="march_swap",
    )(volume, cen, wid, col, opa)


def solution(mesh):
    return jax.shard_map(
        local,
        mesh=mesh,
        in_specs=(P("depth", "imgy", "imgx"), P(), P(), P(), P()),
        out_specs=P(None, "imgy", "depth", "imgx"),
        check_vma=False,
    )
```
